32 devices in a mesh: dom: 4 (over y, x), sub: 8 (over z, core).
Axes of the slice: x: 2, y: 2, z: 4, core: 2. Of those that a mesh axis runs over, the one named last changes fastest.
Arguments:
- positions: float32 [3, 262144], P(None, ('dom', 'sub')), may hold values from -6 to 6
- masses: float32 [262144], P(('dom', 'sub')), may hold values from 0.0002 to 0.002
- velocities: float32 [3, 262144], P(None, ('dom', 'sub')), may hold values from -6 to 6
- destinations: int32 [262144, 1], P(('dom', 'sub')), may hold values from 0 to 7; in each aligned block of 8192 rows (0 to 8191, 8192 to 16383, ...) at most 1280 rows name the same one
- readers: int32 [4, 4, 8, 80], P(None, None, 'sub'), may hold values from 0 to 1, as said below
- near_local: int32 [2, 6144], P(None, ('dom', 'sub')), may hold values from 0 to 79, as said below
- near_remote: int32 [3, 6144], P(None, ('dom', 'sub')), may hold values from 0 to 79, as said below
Outputs:
- acceleration: float32 [3, 327680], P(None, ('dom', 'sub'))
- kicked: float32 [3, 327680], P(None, ('dom', 'sub'))
The draws below stay inside these ranges and needn't reach their ends.
Inputs may be any that keep to these rules, and one draw needn't show every extreme that they name: `destinations`: in the particles of one device, at most 1280 share one destination, and some destination has exactly 1280 in some device. `readers`: no domain reads its own leaves. Of one device's leaves, at most 32 are read by one other domain, and every device has a domain that reads exactly 32 of them. `near_local`: both rows are leaves of the device that owns the pair. `near_remote`: row 0 is a target leaf of the owning device; row 1 a domain other than the owner's; row 2 a leaf of the device at that domain with the owner's sub index that the owner's domain reads.
All inputs are finite; a program needn't handle non-finite values.
Results may differ from the reference program's by a relative error of at most 0.0003.
Values sent between devices are 32-bit elements; how exact they have to be, the bound alone decides.
No kernel may reach another device: no remote copies, remote signals or barrier semaphores. Data moves between devices by JAX's collectives and lax.ppermute only.
A program may use at most 64 MiB of HBM per device.

```python
import math
import jax
import jax.numpy as jnp
import numpy as np
from jax import lax

P_DEV = 8192
LEAF = 128
SLOTS = 32
PAIRS_L = 192
PAIRS_R = 192
CAP = 1280
LEAVES = 80
PARTICLES = 262144
N_DOM = 4
N_SUB = 8
DEVICES = 32


def reader_tables(key):
    base = jax.random.fold_in(key, 17)
    key_count, key_big, key_score = jax.random.split(base, 3)
    owner = jnp.arange(DEVICES, dtype=jnp.int32) // N_SUB
    counts = jax.random.randint(key_count, (DEVICES, N_DOM), 3 * SLOTS // 4, SLOTS + 1, dtype=jnp.int32)
    offset = jax.random.randint(key_big, (DEVICES,), 1, N_DOM, dtype=jnp.int32)
    busiest = (owner + offset) % N_DOM
    peers = jnp.arange(N_DOM, dtype=jnp.int32)
    counts = jnp.where(peers[None, :] == busiest[:, None], SLOTS, counts)
    counts = jnp.where(peers[None, :] == owner[:, None], 0, counts)
    score = jax.random.randint(key_score, (DEVICES, N_DOM, LEAVES), 0, 1 << 20, dtype=jnp.int32)
    score = score * LEAVES + jnp.arange(LEAVES, dtype=jnp.int32)
    ordering = jnp.argsort(jnp.argsort(score, axis=-1, stable=True), axis=-1, stable=True).astype(jnp.int32)
    chosen = (ordering < counts[:, :, None]).astype(jnp.int32)
    return (chosen, ordering, counts)


def draw_readers(key, part):
    chosen, ordering, counts = reader_tables(key)
    return chosen.reshape(N_DOM, N_SUB, N_DOM, LEAVES).transpose(2, 0, 1, 3)


def draw_near_local(key, part):
    key_t, key_s = jax.random.split(jax.random.fold_in(key, 23), 2)
    target = jax.random.randint(key_t, (PAIRS_L * DEVICES,), 0, LEAVES, dtype=jnp.int32)
    source = jax.random.randint(key_s, (PAIRS_L * DEVICES,), 0, LEAVES, dtype=jnp.int32)
    return jnp.stack([target, source], axis=0)


def draw_near_remote(key, part):
    chosen, ordering, counts = reader_tables(key)
    key_t, key_q, key_k = jax.random.split(jax.random.fold_in(key, 29), 3)
    device = jnp.arange(DEVICES, dtype=jnp.int32)[:, None]
    owner = device // N_SUB
    column = device % N_SUB
    target = jax.random.randint(key_t, (DEVICES, PAIRS_R), 0, LEAVES, dtype=jnp.int32)
    offset = jax.random.randint(key_q, (DEVICES, PAIRS_R), 1, N_DOM, dtype=jnp.int32)
    source_dom = (owner + offset) % N_DOM
    sender = source_dom * N_SUB + column
    owner_full = jnp.broadcast_to(owner, (DEVICES, PAIRS_R))
    available = counts[sender, owner_full]
    pick = jax.random.randint(key_k, (DEVICES, PAIRS_R), 0, 1 << 20, dtype=jnp.int32) % available
    ranks = ordering[sender, owner_full]
    leaf_index = jnp.arange(LEAVES, dtype=jnp.int32)
    leaf = jnp.sum(jnp.where(ranks == pick[:, :, None], leaf_index, 0), axis=-1).astype(jnp.int32)
    return jnp.stack([target, source_dom, leaf], axis=0).reshape(3, DEVICES * PAIRS_R)


def shard_levels(rng, dims, pieces, smallest, high):
    factor_of, own = 1.0, jax.random.fold_in(rng, 6)
    for dim, parts in pieces:
        heights = jnp.exp(jax.random.uniform(jax.random.fold_in(own, dim), (parts,), jnp.float32, smallest / len(pieces), high / len(pieces)))
        factor_of = factor_of * jnp.repeat(heights, dims[dim] // parts).reshape([-1 if axis == dim else 1 for axis in range(len(dims))])
    return factor_of


def routed_block(rng, own, number, rows, count, top, reach, skew):
    ranking = jax.random.permutation(rng, count)
    crowded, common = load_shares(count, rows * top, reach, skew, True), load_shares(count, rows * top, reach, skew, False)
    places = jnp.arange(count)

    def named(lengths, offset_by):
        used = int((lengths > 0).sum())
        fixed = max(1, used // 4)
        passed = fixed + (places - fixed + offset_by * (used - fixed)) % max(1, count - fixed)
        return jnp.zeros((count,), jnp.int32).at[ranking[jnp.where(places < fixed, places, passed)]].set(jnp.asarray(lengths, jnp.int32))

    lengths = jnp.where(number % 4 == 0, named(crowded, number // 4), named(common, number - number // 4 - 1))
    mixed = jax.random.permutation(jax.random.fold_in(own, 3), count)
    source_of, taker = mixed[0:count // 2 * 2:2], mixed[1:count // 2 * 2:2]
    room = jnp.minimum(lengths[source_of] - 1, reach - lengths[taker]) // 2
    room = jnp.where((source_of == ranking[0]) | (taker == ranking[0]) | (lengths[taker] == 0), 0, jnp.maximum(room, 0))
    passed = jax.random.randint(jax.random.fold_in(own, 4), (count // 2,), 0, 1 << 20) % (room + 1)
    lengths = lengths.at[source_of].add(-passed).at[taker].add(passed)
    members = jnp.searchsorted(jnp.cumsum(lengths), jnp.arange(rows * top), side="right").astype(jnp.int32)
    listing = members.reshape(top, rows).T
    listing = listing[jax.random.permutation(jax.random.fold_in(own, 1), rows)]
    offset_by = jax.random.randint(jax.random.fold_in(own, 2), (rows, 1), 0, top)
    return jnp.take_along_axis(listing, (jnp.arange(top)[None, :] + offset_by) % top, axis=1)


def load_shares(count, total, limit, lean, full):
    loads = [(1 << 20) // math.isqrt(standing ** lean) + 1 for standing in range(1, count + 1)]
    largest = limit if full else min(limit, max(-(-total // count), total * loads[0] // sum(loads)))
    least = 1 if total - largest >= count - 1 else 0
    given, rest = [largest] + [least] * (count - 1), total - largest - least * (count - 1)
    while rest > 0:
        candidates = [i for i in range(1, count) if given[i] < largest] or [i for i in range(1, count) if given[i] < limit]
        whole, remaining = sum([loads[i] for i in candidates]), rest
        for i in candidates:
            more = min(limit - given[i], max(1, remaining * loads[i] // whole), rest)
            given[i] = given[i] + more
            rest = rest - more
    return np.array(given)


def gaussian(key, dims, spread, bound, pieces=(), kind=jnp.bfloat16):
    level = shard_levels(key, dims, pieces, -0.22, 0.18) if pieces else 1.0
    entries = jax.random.normal(key, dims, jnp.float32) * spread * level
    return jnp.minimum(jnp.maximum(entries, -bound), bound).astype(kind)


def setup_inputs(seed: int = 0) -> dict:
    key_of = jax.random.split(jax.random.key(seed), 8)
    positions = gaussian(key_of[0], (3, PARTICLES), 1.0, 6.0, ((1, 32),), jnp.float32)
    masses = jnp.clip(jnp.exp(math.log(0.002) - 2.3025852 * jax.random.uniform(key_of[1], (PARTICLES,), jnp.float32) ** shard_levels(key_of[1], (PARTICLES,), ((0, 32),), -0.2, 0.2)), 0.0002, 0.002)
    velocities = gaussian(key_of[2], (3, PARTICLES), 1.0, 6.0, ((1, 32),), jnp.float32)
    destinations_keys = jax.random.split(jax.random.fold_in(key_of[3], 1), PARTICLES // P_DEV)
    destinations_turns = jax.random.permutation(jax.random.fold_in(key_of[3], 3), PARTICLES // P_DEV)
    destinations = jax.vmap(lambda own, number: routed_block(jax.random.fold_in(key_of[3], 2), own, number, P_DEV, N_SUB, 1, CAP, 0))(destinations_keys, destinations_turns).reshape((PARTICLES, 1))
    readers = draw_readers(jax.random.fold_in(key_of[7], 71), 0)
    near_local = draw_near_local(jax.random.fold_in(key_of[7], 71), 0)
    near_remote = draw_near_remote(jax.random.fold_in(key_of[7], 71), 0)
    return dict(positions=positions, masses=masses, velocities=velocities, destinations=destinations, readers=readers, near_local=near_local, near_remote=near_remote)


softening = 0.01
gravity = 4.0
kick_time = 0.5

def tile_forces(target_pos, sources):
    delta = sources[:3, :, None, :] - target_pos[:, :, :, None]
    dist_sq = lax.optimization_barrier(jnp.sum(delta * delta, axis=0)) + softening
    inverse = lax.rsqrt(dist_sq)
    weight = sources[3][:, None, :] * inverse * inverse * inverse
    return lax.optimization_barrier(jnp.sum(weight[None] * delta, axis=-1))

def pair_forces(targets, sources, target_ids, source_ids, weights):
    pairs = target_ids.shape[0]
    block = math.gcd(pairs, 64)

    def step(index, total):
        start = index * block
        tgt_block = lax.dynamic_slice_in_dim(target_ids, start, block)
        src_block = lax.dynamic_slice_in_dim(source_ids, start, block)
        wgt_block = lax.dynamic_slice_in_dim(weights, start, block)
        near = tile_forces(jnp.take(targets, tgt_block, axis=1), jnp.take(sources, src_block, axis=1))
        return total.at[:, tgt_block].add(near * wgt_block[None, :, None])
    empty = jnp.zeros((3, targets.shape[1], targets.shape[2]), jnp.float32)
    return lax.fori_loop(0, pairs // block, step, empty)

def regroup_send(state, target):
    onehot = (target[:, None] == jnp.arange(N_SUB, dtype=jnp.int32)[None, :]).astype(jnp.int32)
    before = jnp.cumsum(onehot, axis=0) - onehot
    rank = lax.optimization_barrier(jnp.sum(before * onehot, axis=1)).astype(jnp.int32)
    slot = (target * CAP + rank).astype(jnp.int32)
    table = jnp.zeros((7, N_SUB * CAP), jnp.float32).at[:, slot].set(state)
    return table.reshape(7, N_SUB, CAP)

def reference(positions, masses, velocities, destinations, readers, near_local, near_remote):
    state = jnp.concatenate([positions, masses[None, :], velocities], axis=0)
    state = state.reshape(7, DEVICES, P_DEV).transpose(1, 0, 2)
    targets = destinations[:, 0].reshape(DEVICES, P_DEV)
    sends = jax.vmap(regroup_send)(state, targets)
    regrouped = sends.reshape(N_DOM, N_SUB, 7, N_SUB, CAP).transpose(0, 3, 2, 1, 4)
    regrouped = regrouped.reshape(DEVICES, 7, LEAVES, LEAF)
    local_ids = near_local.reshape(2, DEVICES, PAIRS_L)
    remote_ids = near_remote.reshape(3, DEVICES, PAIRS_R)

    def device_step(device):
        domain = device // N_SUB
        column = device % N_SUB
        mine = lax.dynamic_index_in_dim(regrouped, device, 0, keepdims=False)
        lids = lax.dynamic_index_in_dim(local_ids, device, 1, keepdims=False)
        rids = lax.dynamic_index_in_dim(remote_ids, device, 1, keepdims=False)
        local = pair_forces(mine[:3], mine[:4], lids[0], lids[1], jnp.ones((PAIRS_L,), jnp.float32))
        senders = (jnp.arange(N_DOM, dtype=jnp.int32) * N_SUB + column).astype(jnp.int32)
        remote_src = jnp.take(regrouped[:, :4], senders, axis=0)
        remote_src = remote_src.transpose(1, 0, 2, 3).reshape(4, N_DOM * LEAVES, LEAF)
        table = lax.dynamic_index_in_dim(readers, domain, 0, keepdims=False)
        table = lax.dynamic_index_in_dim(table, column, 1, keepdims=False)
        valid = table[rids[1], rids[2]].astype(jnp.float32)
        source_index = (rids[1] * LEAVES + rids[2]).astype(jnp.int32)
        remote = pair_forces(mine[:3], remote_src, rids[0], source_index, valid)
        accel = gravity * (local + remote)
        accel = jnp.where(mine[3][None] > 0.0, accel, jnp.zeros_like(accel))
        kicked = mine[4:7] + kick_time * accel
        return (accel.reshape(3, LEAVES * LEAF), kicked.reshape(3, LEAVES * LEAF))
    accel_all, kicked_all = lax.map(device_step, jnp.arange(DEVICES, dtype=jnp.int32))
    acceleration = accel_all.transpose(1, 0, 2).reshape(3, DEVICES * LEAVES * LEAF)
    kicked = kicked_all.transpose(1, 0, 2).reshape(3, DEVICES * LEAVES * LEAF)
    return (acceleration, kicked)
```

```python
import functools

import jax
import jax.numpy as jnp
from jax import lax
from jax.experimental import pallas as pl
from jax.experimental.pallas import tpu as pltpu
from jax.sharding import PartitionSpec as P

SLOTS = 32
LEAF = 128
COLS = 8

softening = 0.01
gravity = 4.0
kick_time = 0.5

VMEM_LIMIT = 48 << 20
F32 = jnp.float32
I32 = jnp.int32


def vmem():
    return pl.BlockSpec(memory_space=pltpu.VMEM)


def smem():
    return pl.BlockSpec(memory_space=pltpu.SMEM)


def lane_gather(tile, index):
    return jnp.take_along_axis(tile, index, axis=1, mode="promise_in_bounds")


def regroup_kernel(
    n_sub, leaves, pos_ref, mass_ref, vel_ref, dest_ref, near_ref, far_ref,
    tiles, table, off_ref, cnt_ref, start_ref, perm_ref, leaf_vec, leaf_idx, sem
):
    blocks = dest_ref.shape[0]
    dest = dest_ref[...]
    masks = [dest == e for e in range(n_sub)]
    ones_of = jnp.concatenate([m.astype(F32) for m in masks], axis=0).astype(jnp.bfloat16)
    row = lax.broadcasted_iota(I32, (LEAF, LEAF), 0)
    col = lax.broadcasted_iota(I32, (LEAF, LEAF), 1)
    upper = jnp.where(row <= col, 1.0, 0.0).astype(jnp.bfloat16)
    weights = jnp.concatenate([upper, jnp.ones((LEAF, LEAF), jnp.bfloat16)], axis=1)
    counts = jnp.dot(ones_of, weights, preferred_element_type=F32)
    brow = lax.broadcasted_iota(I32, (blocks, blocks), 0)
    bcol = lax.broadcasted_iota(I32, (blocks, blocks), 1)
    earlier = jnp.where(bcol < brow, 1.0, 0.0).astype(jnp.bfloat16)
    start = jnp.zeros((blocks, LEAF), F32)
    place = jnp.zeros((blocks, LEAF), F32)
    lane64 = lax.broadcasted_iota(I32, (blocks, LEAF), 1)
    leaf_of = jnp.zeros((blocks, LEAF), I32)
    for e in range(n_sub):
        inside = counts[e * blocks:(e + 1) * blocks, :LEAF]
        total = counts[e * blocks:(e + 1) * blocks, LEAF:]
        place = jnp.where(masks[e], inside - 1.0 + start, place)
        offset = jnp.dot(earlier, total.astype(jnp.bfloat16), preferred_element_type=F32).astype(I32)
        off_ref[e] = offset
        cnt_ref[e] = total.astype(I32)
        start_ref[e] = start.astype(I32)
        base = e * (leaves + 1)
        leaf_of = jnp.where(lane64 == e, base + (offset >> 7), leaf_of)
        ends = (offset + total.astype(I32)) >> 7
        leaf_of = jnp.where(lane64 == n_sub + e, base + ends, leaf_of)
        start = start + total
    leaf_vec[...] = leaf_of
    copy = pltpu.make_async_copy(leaf_vec, leaf_idx, sem)
    copy.start()
    perm_ref[...] = place.astype(I32)
    table[...] = jnp.zeros_like(table)
    tiles[...] = jnp.zeros_like(tiles)
    for b in range(blocks):
        lanes = slice(b * LEAF, (b + 1) * LEAF)
        table[b, 0:3, :] = pos_ref[:, lanes]
        table[b, 3:4, :] = mass_ref[b:b + 1, :]
        table[b, 4:7, :] = vel_ref[:, lanes]
    lane = lax.broadcasted_iota(I32, (8, LEAF), 1)
    lane_rows = lax.broadcasted_iota(I32, (16, LEAF), 1).astype(F32).astype(jnp.bfloat16)
    copy.wait()

    def step(b, tails):
        place_row = perm_ref[pl.ds(b, 1), :]
        onehot = jnp.where(row == place_row, 1.0, 0.0).astype(jnp.bfloat16)
        inverse = lax.dot_general(
            lane_rows, onehot, (((1,), (1,)), ((), ())), preferred_element_type=F32
        )[:8].astype(I32)
        ordered = lane_gather(table[b], inverse)
        new = []
        for e in range(n_sub):
            offset = jnp.broadcast_to(off_ref[e, pl.ds(b, 1), :], (8, LEAF))
            count = jnp.broadcast_to(cnt_ref[e, pl.ds(b, 1), :], (8, LEAF))
            first = jnp.broadcast_to(start_ref[e, pl.ds(b, 1), :], (8, LEAF))
            turned = (lane - offset) & (LEAF - 1)
            moved = lane_gather(ordered, (turned + first) & (LEAF - 1))
            low = offset & (LEAF - 1)
            taken = turned < count
            tail = jnp.where(taken & (lane >= low), moved, tails[e])
            tiles[leaf_idx[b, e]] = tail
            fresh = jnp.where(taken & (lane < low), moved, 0.0)
            new.append(jnp.where(low + count >= LEAF, fresh, tail))
        return tuple(new)

    tails = lax.fori_loop(0, blocks, step, (jnp.zeros((8, LEAF), F32),) * n_sub)
    for e in range(n_sub):
        tiles[leaf_idx[blocks - 1, n_sub + e]] = tails[e]
        for l in range(leaves):
            tile = tiles[e * (leaves + 1) + l]
            near_ref[e, 4 * l:4 * l + 4, :] = tile[0:4]
            far_ref[e, 4 * l:4 * l + 4, :] = tile[4:8]


def regroup(positions, masses, velocities, destinations, n_sub, leaves):
    count = positions.shape[1]
    blocks = count // LEAF
    out = jax.ShapeDtypeStruct((n_sub, leaves * 4, LEAF), F32)
    return pl.pallas_call(
        functools.partial(regroup_kernel, n_sub, leaves),
        out_shape=(out, out),
        in_specs=[vmem()] * 4,
        out_specs=(vmem(), vmem()),
        scratch_shapes=[
            pltpu.VMEM((n_sub * (leaves + 1), 8, LEAF), F32),
            pltpu.VMEM((blocks, 8, LEAF), F32),
            pltpu.VMEM((n_sub, blocks, LEAF), I32),
            pltpu.VMEM((n_sub, blocks, LEAF), I32),
            pltpu.VMEM((n_sub, blocks, LEAF), I32),
            pltpu.VMEM((blocks, LEAF), I32),
            pltpu.VMEM((blocks, LEAF), I32),
            pltpu.SMEM((blocks, LEAF), I32),
            pltpu.SemaphoreType.DMA,
        ],
        compiler_params=pltpu.CompilerParams(vmem_limit_bytes=VMEM_LIMIT),
        name="regroup",
    )(positions, masses.reshape(blocks, LEAF), velocities, destinations.reshape(blocks, LEAF))


def plan_kernel(n_dom, leaves, reads_ref, far_ref, me_ref, list_ref, source_ref, valid_ref, lookup):
    me = me_ref[0]
    pairs = far_ref.shape[1]

    def wanted(p, _):
        for k in range(SLOTS):
            list_ref[p, k] = 0

        def leaf(l, taken):
            flag = reads_ref[p, me, l]

            @pl.when(flag > 0)
            def _():
                list_ref[p, taken] = l

            return taken + flag

        def seen(l, before):
            lookup[p, l] = jnp.minimum(before, SLOTS - 1)
            return before + reads_ref[me, p, l]

        lax.fori_loop(0, leaves, leaf, jnp.int32(0))
        lax.fori_loop(0, leaves, seen, jnp.int32(0))
        return 0

    lax.fori_loop(0, n_dom, wanted, 0)

    def pair(i, _):
        q = far_ref[1, i]
        l = far_ref[2, i]
        source_ref[i] = q * SLOTS + lookup[q, l]
        valid_ref[i] = reads_ref[me, q, l].astype(F32)
        return 0

    lax.fori_loop(0, pairs, pair, 0)


def plan(readers, near_remote, my_dom):
    n_dom, leaves = readers.shape[0], readers.shape[3]
    pairs = near_remote.shape[1]
    return pl.pallas_call(
        functools.partial(plan_kernel, n_dom, leaves),
        out_shape=(
            jax.ShapeDtypeStruct((n_dom, SLOTS), I32),
            jax.ShapeDtypeStruct((pairs,), I32),
            jax.ShapeDtypeStruct((pairs,), F32),
        ),
        in_specs=[smem()] * 3,
        out_specs=(smem(), smem(), smem()),
        scratch_shapes=[pltpu.SMEM((n_dom, leaves), I32)],
        name="plan",
    )(readers.reshape(n_dom, n_dom, leaves), near_remote, my_dom.reshape(1))


def bundle_kernel(list_ref, leaf_ref, out_ref):
    n_dom = out_ref.shape[0]

    def step(k, _):
        for p in range(n_dom):
            out_ref[p, k] = leaf_ref[list_ref[p, k]]
        return 0

    lax.fori_loop(0, SLOTS, step, 0, unroll=4)


def bundle(lists, near):
    n_dom = lists.shape[0]
    return pl.pallas_call(
        bundle_kernel,
        out_shape=jax.ShapeDtypeStruct((n_dom, SLOTS, 4, LEAF), F32),
        in_specs=[smem(), vmem()],
        out_specs=vmem(),
        compiler_params=pltpu.CompilerParams(vmem_limit_bytes=VMEM_LIMIT),
        name="bundle",
    )(lists, near.reshape(-1, 4, LEAF))


def columns_of(src_ref, cols_ref):
    rows = src_ref.shape[0]
    for k in range(cols_ref.shape[0]):
        size = min(LEAF, rows - k * LEAF)
        part = src_ref[k * LEAF:k * LEAF + size, :]
        if size < LEAF:
            part = jnp.concatenate([part, jnp.zeros((LEAF - size, LEAF), F32)], axis=0)
        cols_ref[k] = part.T


def pair_loop(pairs, target_of, source_of, weight_of, tgt_ref, cols_ref, acc_ref):
    def step(i, _):
        t = target_of(i)
        s = source_of(i)
        block, first = s >> 5, (s & 31) * 4
        index = [jnp.full((8, LEAF), first + c, I32) for c in range(4)]
        here = [jnp.broadcast_to(tgt_ref[pl.ds(4 * t + c, 1), :], (8, LEAF)) for c in range(3)]
        sums = [jnp.zeros((8, LEAF), F32) for _ in range(3)]
        for g in range(LEAF // 8):
            cols = cols_ref[block, 8 * g:8 * g + 8, :]
            delta = [lane_gather(cols, index[c]) - here[c] for c in range(3)]
            mass = lane_gather(cols, index[3])
            dist = delta[0] * delta[0] + delta[1] * delta[1] + (delta[2] * delta[2] + softening)
            inv = lax.rsqrt(dist)
            weight = (mass * inv) * (inv * inv)
            sums = [sums[c] + weight * delta[c] for c in range(3)]
        scale = weight_of(i)
        for c in range(3):
            part = sums[c] if scale is None else sums[c] * scale
            acc_ref[t, c] += part
        return 0

    lax.fori_loop(0, pairs, step, 0, unroll=2)


def local_kernel(ids_ref, src_ref, out_ref, cols_ref, acc_ref):
    columns_of(src_ref, cols_ref)
    acc_ref[...] = jnp.zeros_like(acc_ref)
    pair_loop(
        ids_ref.shape[1], lambda i: ids_ref[0, i], lambda i: ids_ref[1, i], lambda i: None,
        src_ref, cols_ref, acc_ref,
    )
    for t in range(acc_ref.shape[0]):
        for c in range(3):
            out_ref[4 * t + c:4 * t + c + 1, :] = jnp.sum(acc_ref[t, c], axis=0, keepdims=True)


def local_forces(near_local, near):
    rows = near.shape[0]
    pairs = near_local.shape[1]
    work = pairs * LEAF * LEAF
    return pl.pallas_call(
        local_kernel,
        out_shape=jax.ShapeDtypeStruct((rows, LEAF), F32),
        in_specs=[smem(), vmem()],
        out_specs=vmem(),
        scratch_shapes=[
            pltpu.VMEM((pl.cdiv(rows, LEAF), LEAF, LEAF), F32),
            pltpu.VMEM((rows // 4, 3, 8, LEAF), F32),
        ],
        compiler_params=pltpu.CompilerParams(vmem_limit_bytes=VMEM_LIMIT),
        cost_estimate=pl.CostEstimate(flops=18 * work, transcendentals=work, bytes_accessed=8 * rows * LEAF),
        name="local_forces",
    )(near_local, near)


def remote_kernel(ids_ref, source_ref, valid_ref, tgt_ref, src_ref, local_ref, vel_ref,
                  accel_ref, kicked_ref, cols_ref, acc_ref):
    columns_of(src_ref, cols_ref)
    acc_ref[...] = jnp.zeros_like(acc_ref)
    pair_loop(
        ids_ref.shape[1], lambda i: ids_ref[0, i], lambda i: source_ref[i], lambda i: valid_ref[i],
        tgt_ref, cols_ref, acc_ref,
    )
    for t in range(acc_ref.shape[0]):
        used = tgt_ref[4 * t + 3:4 * t + 4, :] > 0.0
        lanes = slice(t * LEAF, (t + 1) * LEAF)
        for c in range(3):
            row = slice(4 * t + c, 4 * t + c + 1)
            total = local_ref[row, :] + jnp.sum(acc_ref[t, c], axis=0, keepdims=True)
            accel = jnp.where(used, gravity * total, 0.0)
            accel_ref[c:c + 1, lanes] = accel
            kicked_ref[c:c + 1, lanes] = vel_ref[row, :] + kick_time * accel


def remote_forces(near_remote, source, valid, near, arrived, local, vel):
    rows = near.shape[0]
    pairs = near_remote.shape[1]
    work = pairs * LEAF * LEAF
    out = jax.ShapeDtypeStruct((3, rows // 4 * LEAF), F32)
    return pl.pallas_call(
        remote_kernel,
        out_shape=(out, out),
        in_specs=[smem(), smem(), smem(), vmem(), vmem(), vmem(), vmem()],
        out_specs=(vmem(), vmem()),
        scratch_shapes=[
            pltpu.VMEM((pl.cdiv(arrived.shape[0], LEAF), LEAF, LEAF), F32),
            pltpu.VMEM((rows // 4, 3, 8, LEAF), F32),
        ],
        compiler_params=pltpu.CompilerParams(vmem_limit_bytes=VMEM_LIMIT),
        cost_estimate=pl.CostEstimate(flops=18 * work, transcendentals=work, bytes_accessed=24 * rows * LEAF),
        name="remote_forces",
    )(near_remote, source, valid, near, arrived, local, vel)


def on_device(positions, masses, velocities, destinations, readers, near_local, near_remote):
    n_sub = lax.axis_size("sub")
    n_dom = lax.axis_size("dom")
    count = positions.shape[1]
    capacity = 5 * count // (4 * n_sub)
    leaves = capacity // LEAF
    near, far = regroup(positions, masses, velocities, destinations, n_sub, leaves)
    near = lax.all_to_all(near, "sub", split_axis=0, concat_axis=0, tiled=True)
    lists, source, valid = plan(readers, near_remote, lax.axis_index("dom").astype(I32))
    near = near.reshape(n_sub * leaves * 4, LEAF)
    packed = bundle(lists, near)
    arrived = lax.all_to_all(packed, "dom", split_axis=0, concat_axis=0, tiled=True)
    far = lax.all_to_all(far, "sub", split_axis=0, concat_axis=0, tiled=True)
    local = local_forces(near_local, near)
    return remote_forces(
        near_remote, source, valid, near, arrived.reshape(n_dom * SLOTS * 4, LEAF), local,
        far.reshape(n_sub * leaves * 4, LEAF),
    )


def solution(mesh):
    in_specs = (
        P(None, ("dom", "sub")),
        P(("dom", "sub")),
        P(None, ("dom", "sub")),
        P(("dom", "sub"), None),
        P(None, None, "sub", None),
        P(None, ("dom", "sub")),
        P(None, ("dom", "sub")),
    )
    out_specs = (P(None, ("dom", "sub")), P(None, ("dom", "sub")))
    return jax.shard_map(
        on_device, mesh=mesh, in_specs=in_specs, out_specs=out_specs, check_vma=False
    )
```

```python
import functools

import jax
import jax.numpy as jnp
from jax import lax
from jax.experimental import pallas as pl
from jax.experimental.pallas import tpu as pltpu
from jax.sharding import PartitionSpec as P

SLOTS = 32
LEAF = 128
ROWS = 4 * SLOTS

softening = 0.01
gravity = 4.0
kick_time = 0.5

VMEM_LIMIT = 48 << 20
F32 = jnp.float32
I32 = jnp.int32
BF16 = jnp.bfloat16


def vmem():
    return pl.BlockSpec(memory_space=pltpu.VMEM)


def smem():
    return pl.BlockSpec(memory_space=pltpu.SMEM)


def anywhere():
    return pl.BlockSpec(memory_space=pl.ANY)


def params():
    return pltpu.CompilerParams(vmem_limit_bytes=VMEM_LIMIT)


def lane_gather(tile, index):
    return jnp.take_along_axis(tile, index, axis=1, mode="promise_in_bounds")


def iota(shape, dim):
    return lax.broadcasted_iota(I32, shape, dim)


def as_bf16(condition):
    return jnp.where(condition, 1.0, 0.0).astype(BF16)


def plan_reads(n_dom, reads_ref, list_ref, lookup_ref):
    me = lax.axis_index("dom")
    leaves = reads_ref.shape[2]
    lower = as_bf16(iota((leaves, leaves), 0) < iota((leaves, leaves), 1))
    wanted = jnp.concatenate([reads_ref[p, pl.ds(me, 1), :] for p in range(n_dom)], axis=0)
    flags = jnp.concatenate([wanted, reads_ref[me]], axis=0).astype(F32)
    place = jnp.dot(flags.astype(BF16), lower, preferred_element_type=F32).astype(I32)
    lookup_ref[...] = jnp.minimum(place[n_dom:], SLOTS - 1)
    slot = iota((SLOTS, leaves), 0)
    leaf = iota((SLOTS, leaves), 1)
    lane = iota((SLOTS, LEAF), 1)
    lists = jnp.zeros((SLOTS, LEAF), I32)
    for p in range(n_dom):
        hit = (place[p:p + 1] == slot) & (wanted[p:p + 1] > 0)
        lists = jnp.where(lane == p, jnp.sum(jnp.where(hit, leaf, 0), axis=1, keepdims=True), lists)
    list_ref[...] = lists


def regroup_kernel(
    n_sub, n_dom, leaves, pos_hbm, mass_hbm, vel_hbm, dest_hbm, reads_ref,
    near_ref, far_ref, list_ref, lookup_ref,
    pos_ref, mass_ref, vel_ref, dest_ref, tiles, table, ordered,
    off_ref, cnt_ref, start_ref, perm_ref, leaf_vec, leaf_idx, sems
):
    blocks = dest_ref.shape[0]
    loads = [
        pltpu.make_async_copy(source, target, sems.at[n])
        for n, (source, target) in enumerate(
            [(dest_hbm, dest_ref), (pos_hbm, pos_ref), (mass_hbm, mass_ref), (vel_hbm, vel_ref)]
        )
    ]
    for load in loads:
        load.start()
    plan_reads(n_dom, reads_ref, list_ref, lookup_ref)
    tiles[...] = jnp.zeros_like(tiles)
    row = iota((LEAF, LEAF), 0)
    weights = jnp.concatenate([as_bf16(row <= iota((LEAF, LEAF), 1)), jnp.ones((LEAF, LEAF), BF16)], axis=1)
    earlier = as_bf16(iota((blocks, blocks), 1) < iota((blocks, blocks), 0))
    lane64 = iota((blocks, LEAF), 1)
    loads[0].wait()
    dest = dest_ref[...]
    masks = [dest == e for e in range(n_sub)]
    ones_of = jnp.concatenate([as_bf16(m) for m in masks], axis=0)
    counts = jnp.dot(ones_of, weights, preferred_element_type=F32)
    start = jnp.zeros((blocks, LEAF), F32)
    place = jnp.zeros((blocks, LEAF), F32)
    leaf_of = jnp.zeros((blocks, LEAF), I32)
    for e in range(n_sub):
        inside = counts[e * blocks:(e + 1) * blocks, :LEAF]
        total = counts[e * blocks:(e + 1) * blocks, LEAF:]
        place = jnp.where(masks[e], inside - 1.0 + start, place)
        offset = jnp.dot(earlier, total.astype(BF16), preferred_element_type=F32).astype(I32)
        count = total.astype(I32)
        off_ref[e] = offset
        cnt_ref[e] = count
        start_ref[e] = start.astype(I32)
        base = e * (leaves + 1)
        leaf_of = jnp.where(lane64 == e, base + (offset >> 7), leaf_of)
        leaf_of = jnp.where(lane64 == n_sub + e, base + ((offset + count) >> 7), leaf_of)
        start = start + total
    leaf_vec[...] = leaf_of
    copy = pltpu.make_async_copy(leaf_vec, leaf_idx, sems.at[4])
    copy.start()
    perm_ref[...] = place.astype(I32)
    for load in loads[1:]:
        load.wait()
    table[:, 7:8, :] = jnp.zeros((blocks, 1, LEAF), F32)
    for b in range(blocks):
        lanes = slice(b * LEAF, (b + 1) * LEAF)
        table[b, 0:3, :] = pos_ref[:, lanes]
        table[b, 3:4, :] = mass_ref[b:b + 1, :]
        table[b, 4:7, :] = vel_ref[:, lanes]
    lane = iota((8, LEAF), 1)
    lane_rows = iota((16, LEAF), 1).astype(F32).astype(BF16)

    def order(b, _):
        onehot = as_bf16(row == perm_ref[pl.ds(b, 1), :])
        inverse = lax.dot_general(
            lane_rows, onehot, (((1,), (1,)), ((), ())), preferred_element_type=F32
        )[:8].astype(I32)
        ordered[b] = lane_gather(table[b], inverse)
        return 0

    lax.fori_loop(0, blocks, order, 0, unroll=8)
    copy.wait()

    def step(b, tails):
        block = ordered[b]
        new = []
        for e in range(n_sub):
            offset = jnp.broadcast_to(off_ref[e, pl.ds(b, 1), :], (8, LEAF))
            count = jnp.broadcast_to(cnt_ref[e, pl.ds(b, 1), :], (8, LEAF))
            first = jnp.broadcast_to(start_ref[e, pl.ds(b, 1), :], (8, LEAF))
            turned = (lane - offset) & (LEAF - 1)
            moved = lane_gather(block, (turned + first) & (LEAF - 1))
            low = offset & (LEAF - 1)
            taken = turned < count
            tail = jnp.where(taken & (lane >= low), moved, tails[e])
            tiles[leaf_idx[b, e]] = tail
            fresh = jnp.where(taken & (lane < low), moved, 0.0)
            new.append(jnp.where(low + count >= LEAF, fresh, tail))
        return tuple(new)

    tails = lax.fori_loop(0, blocks, step, (jnp.zeros((8, LEAF), F32),) * n_sub, unroll=4)
    for e in range(n_sub):
        tiles[leaf_idx[blocks - 1, n_sub + e]] = tails[e]
        for l in range(leaves):
            tile = tiles[e * (leaves + 1) + l]
            near_ref[e, 4 * l:4 * l + 4, :] = tile[0:4]
            far_ref[e, 4 * l:4 * l + 4, :] = tile[4:8]


def regroup(positions, masses, velocities, destinations, reads, n_sub, leaves):
    count = positions.shape[1]
    blocks = count // LEAF
    n_dom = reads.shape[0]
    out = jax.ShapeDtypeStruct((n_sub, leaves * 4, LEAF), F32)
    return pl.pallas_call(
        functools.partial(regroup_kernel, n_sub, n_dom, leaves),
        out_shape=(
            out,
            out,
            jax.ShapeDtypeStruct((SLOTS, LEAF), I32),
            jax.ShapeDtypeStruct((n_dom, reads.shape[2]), I32),
        ),
        in_specs=[anywhere()] * 4 + [vmem()],
        out_specs=(vmem(),) * 4,
        scratch_shapes=[
            pltpu.VMEM((3, count), F32),
            pltpu.VMEM((blocks, LEAF), F32),
            pltpu.VMEM((3, count), F32),
            pltpu.VMEM((blocks, LEAF), I32),
            pltpu.VMEM((n_sub * (leaves + 1), 8, LEAF), F32),
            pltpu.VMEM((blocks, 8, LEAF), F32),
            pltpu.VMEM((blocks, 8, LEAF), F32),
            pltpu.VMEM((n_sub, blocks, LEAF), I32),
            pltpu.VMEM((n_sub, blocks, LEAF), I32),
            pltpu.VMEM((n_sub, blocks, LEAF), I32),
            pltpu.VMEM((blocks, LEAF), I32),
            pltpu.VMEM((blocks, LEAF), I32),
            pltpu.SMEM((blocks, LEAF), I32),
            pltpu.SemaphoreType.DMA((5,)),
        ],
        compiler_params=params(),
        name="regroup",
    )(positions, masses.reshape(blocks, LEAF), velocities, destinations.reshape(blocks, LEAF), reads)


def bundle_kernel(n_dom, list_ref, leaf_hbm, *rest):
    outs, sems = rest[:n_dom - 1], rest[n_dom - 1]
    me = lax.axis_index("dom")
    for k in range(1, n_dom):
        for slot in range(SLOTS):
            leaf = list_ref[slot, me ^ k]
            pltpu.make_async_copy(leaf_hbm.at[leaf], outs[k - 1].at[slot], sems.at[k - 1]).start()
    for k in range(1, n_dom):
        pltpu.make_async_copy(outs[k - 1], outs[k - 1], sems.at[k - 1]).wait()


def bundle(lists, near, n_dom):
    return pl.pallas_call(
        functools.partial(bundle_kernel, n_dom),
        out_shape=(jax.ShapeDtypeStruct((SLOTS, 4, LEAF), F32),) * (n_dom - 1),
        in_specs=[smem(), anywhere()],
        out_specs=(anywhere(),) * (n_dom - 1),
        scratch_shapes=[pltpu.SemaphoreType.DMA((n_dom - 1,))],
        compiler_params=params(),
        name="bundle",
    )(lists, near)


def spread_sources(src_refs, wide_ref):
    group = iota((8, LEAF), 1) & ~15

    def spread(k, _):
        h = 0
        for src_ref in src_refs:
            for r in range(0, src_ref.shape[0], 8):
                wide_ref[k, h] = lane_gather(src_ref[r:r + 8, :], group + k)
                h += 1
        return 0

    lax.fori_loop(0, 16, spread, 0)


def pair_loop(pairs, target_of, source_of, weight_of, here_ref, wide_ref, acc_ref):
    def step(i, _):
        t = target_of(i)
        s = source_of(i)
        h, first = s >> 1, (s & 1) * 4
        here = [here_ref[t, c] for c in range(3)]
        sums = None
        for k in range(16):
            there = [jnp.broadcast_to(wide_ref[k, h, pl.ds(first + c, 1), :], (8, LEAF)) for c in range(4)]
            delta = [there[c] - here[c] for c in range(3)]
            dist = delta[0] * delta[0] + delta[1] * delta[1] + (delta[2] * delta[2] + softening)
            inv = lax.rsqrt(dist)
            weight = (there[3] * inv) * (inv * inv)
            terms = [weight * delta[c] for c in range(3)]
            sums = terms if sums is None else [sums[c] + terms[c] for c in range(3)]
        scale = weight_of(i)
        for c in range(3):
            acc_ref[t, c] += sums[c] if scale is None else sums[c] * scale
        return 0

    lax.fori_loop(0, pairs, step, 0, unroll=4)


def local_kernel(ids_ref, src_ref, acc_ref, here_ref, wide_ref):
    spread_sources([src_ref], wide_ref)
    leaves = acc_ref.shape[0]
    fold = iota((8, LEAF), 0) * 16 + (iota((8, LEAF), 1) & 15)
    batch = 8 if leaves % 8 == 0 else 1

    def pack(j, _):
        for u in range(batch):
            for c in range(3):
                line = src_ref[pl.ds(4 * (j * batch + u) + c, 1), :]
                here_ref[j * batch + u, c] = lane_gather(jnp.broadcast_to(line, (8, LEAF)), fold)
        return 0

    lax.fori_loop(0, leaves // batch, pack, 0)
    acc_ref[...] = jnp.zeros_like(acc_ref)
    pair_loop(
        ids_ref.shape[1], lambda i: ids_ref[0, i], lambda i: ids_ref[1, i], lambda i: None,
        here_ref, wide_ref, acc_ref,
    )


def local_forces(near_local, near):
    rows = near.shape[0]
    leaves = rows // 4
    work = near_local.shape[1] * LEAF * LEAF
    return pl.pallas_call(
        local_kernel,
        out_shape=(
            jax.ShapeDtypeStruct((leaves, 4, 8, LEAF), F32),
            jax.ShapeDtypeStruct((leaves, 3, 8, LEAF), F32),
        ),
        in_specs=[smem(), vmem()],
        out_specs=(vmem(), vmem()),
        scratch_shapes=[pltpu.VMEM((16, rows // 8, 8, LEAF), F32)],
        compiler_params=params(),
        cost_estimate=pl.CostEstimate(flops=18 * work, transcendentals=work, bytes_accessed=8 * rows * LEAF),
        name="local_forces",
    )(near_local, near)


def three_parts(x):
    high = x.astype(BF16)
    rest = x - high.astype(F32)
    middle = rest.astype(BF16)
    return [high, middle, (rest - middle.astype(F32)).astype(BF16)]


def unpack_sums(acc_refs, leaves):
    source, target = iota((LEAF, LEAF), 0), iota((LEAF, LEAF), 1)
    parts, picks = [], []
    for s in range(8):
        lines = [ref.reshape(leaves * 32, LEAF)[pl.ds(s, leaves * 4, stride=8), :] for ref in acc_refs]
        pick = as_bf16(((source & 15) == (target & 15)) & ((target >> 4) == s))
        parts += three_parts(sum(lines[1:], lines[0]))
        picks += [pick] * 3
    return jnp.dot(
        jnp.concatenate(parts, axis=1), jnp.concatenate(picks, axis=0), preferred_element_type=F32
    )


def remote_kernel(n_dom, ids_ref, lookup_ref, reads_ref, tgt_ref, vel_ref, local_ref, here_ref, *rest):
    src_refs = rest[:n_dom - 1]
    accel_ref, kicked_ref, wide_ref, acc_ref = rest[n_dom - 1:]
    me = lax.axis_index("dom")
    spread_sources(src_refs, wide_ref)
    acc_ref[...] = jnp.zeros_like(acc_ref)

    def source_of(i):
        q = ids_ref[1, i]
        return jnp.maximum((q ^ me) - 1, 0) * SLOTS + lookup_ref[q, ids_ref[2, i]]

    def weight_of(i):
        return reads_ref[me, ids_ref[1, i], ids_ref[2, i]].astype(F32)

    pair_loop(ids_ref.shape[1], lambda i: ids_ref[0, i], source_of, weight_of, here_ref, wide_ref, acc_ref)
    leaves = acc_ref.shape[0]
    total = gravity * unpack_sums([local_ref, acc_ref], leaves)
    first = iota((8, LEAF), 0) < 4
    for h in range(leaves // 2):
        rows = slice(8 * h, 8 * h + 8)
        mass = [jnp.broadcast_to(tgt_ref[8 * h + r:8 * h + r + 1, :], (8, LEAF)) for r in (3, 7)]
        accel = jnp.where(jnp.where(first, mass[0], mass[1]) > 0.0, total[rows], 0.0)
        kicked = vel_ref[rows, :] + kick_time * accel
        for u in range(2):
            lanes = slice((2 * h + u) * LEAF, (2 * h + u + 1) * LEAF)
            accel_ref[:, lanes] = accel[4 * u:4 * u + 3]
            kicked_ref[:, lanes] = kicked[4 * u:4 * u + 3]


def remote_forces(near_remote, lookup, reads, near, vel, local, here, arrived):
    n_dom = reads.shape[0]
    rows = near.shape[0]
    leaves = rows // 4
    work = near_remote.shape[1] * LEAF * LEAF
    out = jax.ShapeDtypeStruct((3, leaves * LEAF), F32)
    return pl.pallas_call(
        functools.partial(remote_kernel, n_dom),
        out_shape=(out, out),
        in_specs=[smem()] * 3 + [vmem()] * (3 + n_dom),
        out_specs=(vmem(), vmem()),
        scratch_shapes=[
            pltpu.VMEM((16, (n_dom - 1) * ROWS // 8, 8, LEAF), F32),
            pltpu.VMEM((leaves, 4, 8, LEAF), F32),
        ],
        compiler_params=params(),
        cost_estimate=pl.CostEstimate(flops=18 * work, transcendentals=work, bytes_accessed=24 * rows * LEAF),
        name="remote_forces",
    )(near_remote, lookup, reads, near, vel, local, here, *arrived)


def on_device(positions, masses, velocities, destinations, readers, near_local, near_remote):
    n_sub = lax.axis_size("sub")
    n_dom = lax.axis_size("dom")
    count = positions.shape[1]
    capacity = 5 * count // (4 * n_sub)
    leaves = capacity // LEAF
    reads = readers.reshape(n_dom, n_dom, readers.shape[3])
    near, far, lists, lookup = regroup(positions, masses, velocities, destinations, reads, n_sub, leaves)
    near = lax.all_to_all(near, "sub", split_axis=0, concat_axis=0, tiled=True)
    packed = bundle(lists, near.reshape(n_sub * leaves, 4, LEAF), n_dom)
    arrived = [
        lax.ppermute(packed[k - 1], "dom", [(i, i ^ k) for i in range(n_dom)]).reshape(ROWS, LEAF)
        for k in range(1, n_dom)
    ]
    far = lax.all_to_all(far, "sub", split_axis=0, concat_axis=0, tiled=True)
    near = near.reshape(n_sub * leaves * 4, LEAF)
    local, here = local_forces(near_local, near)
    return remote_forces(
        near_remote, lookup, reads, near, far.reshape(n_sub * leaves * 4, LEAF), local, here, arrived
    )


def solution(mesh):
    in_specs = (
        P(None, ("dom", "sub")),
        P(("dom", "sub")),
        P(None, ("dom", "sub")),
        P(("dom", "sub"), None),
        P(None, None, "sub", None),
        P(None, ("dom", "sub")),
        P(None, ("dom", "sub")),
    )
    out_specs = (P(None, ("dom", "sub")), P(None, ("dom", "sub")))
    return jax.shard_map(
        on_device, mesh=mesh, in_specs=in_specs, out_specs=out_specs, check_vma=False
    )
```

```python
import functools

import jax
import jax.numpy as jnp
from jax import lax
from jax.experimental import pallas as pl
from jax.experimental.pallas import tpu as pltpu
from jax.sharding import PartitionSpec as P

SLOTS = 32
LEAF = 128

softening = 0.01
gravity = 4.0
kick_time = 0.5

VMEM_LIMIT = 48 << 20
F32 = jnp.float32
I32 = jnp.int32
BF16 = jnp.bfloat16


def vmem():
    return pl.BlockSpec(memory_space=pltpu.VMEM)


def smem():
    return pl.BlockSpec(memory_space=pltpu.SMEM)


def hbm():
    return pl.BlockSpec(memory_space=pltpu.HBM)


def in_hbm(*arrays):
    return [pltpu.with_memory_space_constraint(x, pltpu.MemorySpace.HBM) for x in arrays]


def params():
    return pltpu.CompilerParams(vmem_limit_bytes=VMEM_LIMIT)


def lane_gather(tile, index):
    return jnp.take_along_axis(tile, index, axis=1, mode="promise_in_bounds")


def iota(shape, dim):
    return lax.broadcasted_iota(I32, shape, dim)


def as_bf16(condition):
    return jnp.where(condition, 1.0, 0.0).astype(BF16)


def plan_reads(n_dom, reads_ref, list_ref, lookup_ref):
    leaves = reads_ref.shape[2]
    lower = as_bf16(iota((leaves, leaves), 0) < iota((leaves, leaves), 1))
    wanted = reads_ref[lax.axis_index("dom")]
    flags = wanted.astype(F32).astype(BF16)
    place = jnp.dot(flags, lower, preferred_element_type=F32).astype(I32)
    lookup_ref[...] = jnp.minimum(place, SLOTS - 1)
    slot = iota((SLOTS, leaves), 0)
    leaf = iota((SLOTS, leaves), 1)
    lane = iota((SLOTS, LEAF), 1)
    lists = jnp.zeros((SLOTS, LEAF), I32)
    for q in range(n_dom):
        hit = (place[q:q + 1] == slot) & (wanted[q:q + 1] > 0)
        lists = jnp.where(lane == q, jnp.sum(jnp.where(hit, leaf, 0), axis=1, keepdims=True), lists)
    list_ref[...] = lists


def regroup_kernel(
    n_sub, n_dom, leaves, pos_hbm, mass_hbm, vel_hbm, dest_hbm, reads_hbm,
    near_ref, far_ref, list_ref, lookup_ref,
    pos_ref, mass_ref, vel_ref, dest_ref, reads_ref, tiles, table, ordered,
    off_ref, cnt_ref, start_ref, perm_ref, leaf_vec, leaf_idx, sems
):
    blocks = dest_ref.shape[0]
    loads = [
        pltpu.make_async_copy(source, target, sems.at[n])
        for n, (source, target) in enumerate(
            [(dest_hbm, dest_ref), (reads_hbm, reads_ref), (pos_hbm, pos_ref), (mass_hbm, mass_ref), (vel_hbm, vel_ref)]
        )
    ]
    for load in loads:
        load.start()
    tiles[...] = jnp.zeros_like(tiles)
    row = iota((LEAF, LEAF), 0)
    weights = jnp.concatenate([as_bf16(row <= iota((LEAF, LEAF), 1)), jnp.ones((LEAF, LEAF), BF16)], axis=1)
    earlier = as_bf16(iota((blocks, blocks), 1) < iota((blocks, blocks), 0))
    lane64 = iota((blocks, LEAF), 1)
    loads[0].wait()
    dest = dest_ref[...]
    masks = [dest == e for e in range(n_sub)]
    ones_of = jnp.concatenate([as_bf16(m) for m in masks], axis=0)
    counts = jnp.dot(ones_of, weights, preferred_element_type=F32)
    start = jnp.zeros((blocks, LEAF), F32)
    place = jnp.zeros((blocks, LEAF), F32)
    leaf_of = jnp.zeros((blocks, LEAF), I32)
    for e in range(n_sub):
        inside = counts[e * blocks:(e + 1) * blocks, :LEAF]
        total = counts[e * blocks:(e + 1) * blocks, LEAF:]
        place = jnp.where(masks[e], inside - 1.0 + start, place)
        offset = jnp.dot(earlier, total.astype(BF16), preferred_element_type=F32).astype(I32)
        count = total.astype(I32)
        off_ref[e] = offset
        cnt_ref[e] = count
        start_ref[e] = start.astype(I32)
        base = e * (leaves + 1)
        leaf_of = jnp.where(lane64 == e, base + (offset >> 7), leaf_of)
        leaf_of = jnp.where(lane64 == n_sub + e, base + ((offset + count) >> 7), leaf_of)
        start = start + total
    leaf_vec[...] = leaf_of
    copy = pltpu.make_async_copy(leaf_vec, leaf_idx, sems.at[5])
    copy.start()
    perm_ref[...] = place.astype(I32)
    for load in loads[1:]:
        load.wait()
    plan_reads(n_dom, reads_ref, list_ref, lookup_ref)
    table[:, 7:8, :] = jnp.zeros((blocks, 1, LEAF), F32)
    for b in range(blocks):
        lanes = slice(b * LEAF, (b + 1) * LEAF)
        table[b, 0:3, :] = pos_ref[:, lanes]
        table[b, 3:4, :] = mass_ref[b:b + 1, :]
        table[b, 4:7, :] = vel_ref[:, lanes]
    lane = iota((8, LEAF), 1)
    lane_rows = iota((16, LEAF), 1).astype(F32).astype(BF16)

    def order(b, _):
        onehot = as_bf16(row == perm_ref[pl.ds(b, 1), :])
        inverse = lax.dot_general(
            lane_rows, onehot, (((1,), (1,)), ((), ())), preferred_element_type=F32
        )[:8].astype(I32)
        ordered[b] = lane_gather(table[b], inverse)
        return 0

    lax.fori_loop(0, blocks, order, 0, unroll=32)
    copy.wait()

    def step(b, tails):
        block = ordered[b]
        new = []
        for e in range(n_sub):
            offset = jnp.broadcast_to(off_ref[e, pl.ds(b, 1), :], (8, LEAF))
            count = jnp.broadcast_to(cnt_ref[e, pl.ds(b, 1), :], (8, LEAF))
            first = jnp.broadcast_to(start_ref[e, pl.ds(b, 1), :], (8, LEAF))
            turned = (lane - offset) & (LEAF - 1)
            moved = lane_gather(block, (turned + first) & (LEAF - 1))
            low = offset & (LEAF - 1)
            taken = turned < count
            tail = jnp.where(taken & (lane >= low), moved, tails[e])
            tiles[leaf_idx[b, e]] = tail
            fresh = jnp.where(taken & (lane < low), moved, 0.0)
            new.append(jnp.where(low + count >= LEAF, fresh, tail))
        return tuple(new)

    tails = lax.fori_loop(0, blocks, step, (jnp.zeros((8, LEAF), F32),) * n_sub, unroll=8)
    for e in range(n_sub):
        tiles[leaf_idx[blocks - 1, n_sub + e]] = tails[e]
        for l in range(leaves):
            tile = tiles[e * (leaves + 1) + l]
            near_ref[e, 4 * l:4 * l + 4, :] = tile[0:4]
            far_ref[e, 4 * l:4 * l + 4, :] = tile[4:8]


def regroup(positions, masses, velocities, destinations, reads, n_sub, leaves):
    count = positions.shape[1]
    blocks = count // LEAF
    n_dom = reads.shape[0]
    out = jax.ShapeDtypeStruct((n_sub, leaves * 4, LEAF), F32)
    return pl.pallas_call(
        functools.partial(regroup_kernel, n_sub, n_dom, leaves),
        out_shape=(
            out,
            out,
            jax.ShapeDtypeStruct((SLOTS, LEAF), I32),
            jax.ShapeDtypeStruct((n_dom, reads.shape[2]), I32),
        ),
        in_specs=[hbm()] * 5,
        out_specs=(vmem(),) * 4,
        scratch_shapes=[
            pltpu.VMEM((3, count), F32),
            pltpu.VMEM((blocks, LEAF), F32),
            pltpu.VMEM((3, count), F32),
            pltpu.VMEM((blocks, LEAF), I32),
            pltpu.VMEM(reads.shape, I32),
            pltpu.VMEM((n_sub * (leaves + 1), 8, LEAF), F32),
            pltpu.VMEM((blocks, 8, LEAF), F32),
            pltpu.VMEM((blocks, 8, LEAF), F32),
            pltpu.VMEM((n_sub, blocks, LEAF), I32),
            pltpu.VMEM((n_sub, blocks, LEAF), I32),
            pltpu.VMEM((n_sub, blocks, LEAF), I32),
            pltpu.VMEM((blocks, LEAF), I32),
            pltpu.VMEM((blocks, LEAF), I32),
            pltpu.SMEM((blocks, LEAF), I32),
            pltpu.SemaphoreType.DMA((6,)),
        ],
        compiler_params=params(),
        name="regroup",
    )(*in_hbm(positions, masses.reshape(blocks, LEAF), velocities, destinations.reshape(blocks, LEAF), reads))


def spread_tiles(tiles, wide_ref):
    group = iota((8, LEAF), 1) & ~15
    for k in range(16):
        for h, tile in enumerate(tiles):
            wide_ref[k, h] = lane_gather(tile(), group + k)


def pair_loop(pairs, target_of, source_of, weight_of, here_ref, wide_ref, acc_ref):
    def step(i, _):
        t = target_of(i)
        s = source_of(i)
        h, first = s >> 1, (s & 1) * 4
        here = [here_ref[t, c] for c in range(3)]
        sums = None
        for k in range(16):
            there = [jnp.broadcast_to(wide_ref[k, h, pl.ds(first + c, 1), :], (8, LEAF)) for c in range(4)]
            delta = [there[c] - here[c] for c in range(3)]
            dist = delta[0] * delta[0] + delta[1] * delta[1] + (delta[2] * delta[2] + softening)
            inv = lax.rsqrt(dist)
            weight = (there[3] * inv) * (inv * inv)
            terms = [weight * delta[c] for c in range(3)]
            sums = terms if sums is None else [sums[c] + terms[c] for c in range(3)]
        scale = weight_of(i)
        for c in range(3):
            acc_ref[t, c] += sums[c] if scale is None else sums[c] * scale
        return 0

    lax.fori_loop(0, pairs, step, 0, unroll=4)


def local_kernel(ids_hbm, src_ref, acc_ref, here_ref, ids_ref, wide_ref, sem):
    load = pltpu.make_async_copy(ids_hbm, ids_ref, sem)
    load.start()
    leaves = acc_ref.shape[0]
    spread_tiles([functools.partial(src_ref.__getitem__, pl.ds(8 * h, 8)) for h in range(leaves // 2)], wide_ref)
    fold = iota((8, LEAF), 0) * 16 + (iota((8, LEAF), 1) & 15)
    for t in range(leaves):
        for c in range(3):
            line = src_ref[4 * t + c:4 * t + c + 1, :]
            here_ref[t, c] = lane_gather(jnp.broadcast_to(line, (8, LEAF)), fold)
    acc_ref[...] = jnp.zeros_like(acc_ref)
    load.wait()
    pair_loop(
        ids_ref.shape[1], lambda i: ids_ref[0, i], lambda i: ids_ref[1, i], lambda i: None,
        here_ref, wide_ref, acc_ref,
    )


def local_forces(near_local, near):
    rows = near.shape[0]
    leaves = rows // 4
    work = near_local.shape[1] * LEAF * LEAF
    return pl.pallas_call(
        local_kernel,
        out_shape=(
            jax.ShapeDtypeStruct((leaves, 4, 8, LEAF), F32),
            jax.ShapeDtypeStruct((leaves, 3, 8, LEAF), F32),
        ),
        in_specs=[hbm(), vmem()],
        out_specs=(vmem(), vmem()),
        scratch_shapes=[
            pltpu.SMEM(near_local.shape, I32),
            pltpu.VMEM((16, rows // 8, 8, LEAF), F32),
            pltpu.SemaphoreType.DMA,
        ],
        compiler_params=params(),
        cost_estimate=pl.CostEstimate(flops=18 * work, transcendentals=work, bytes_accessed=8 * rows * LEAF),
        name="local_forces",
    )(*in_hbm(near_local), near)


def three_parts(x):
    high = x.astype(BF16)
    rest = x - high.astype(F32)
    middle = rest.astype(BF16)
    return [high, middle, (rest - middle.astype(F32)).astype(BF16)]


def unpack_sums(acc_refs, leaves):
    source, target = iota((LEAF, LEAF), 0), iota((LEAF, LEAF), 1)
    parts, picks = [], []
    for s in range(8):
        lines = [ref.reshape(leaves * 32, LEAF)[pl.ds(s, leaves * 4, stride=8), :] for ref in acc_refs]
        pick = as_bf16(((source & 15) == (target & 15)) & ((target >> 4) == s))
        parts += three_parts(sum(lines[1:], lines[0]))
        picks += [pick] * 3
    return jnp.dot(
        jnp.concatenate(parts, axis=1), jnp.concatenate(picks, axis=0), preferred_element_type=F32
    )


def remote_kernel(
    n_dom, ids_hbm, lookup_hbm, list_hbm, reads_hbm, tgt_ref, vel_ref, local_ref, here_ref, *rest
):
    src_refs = rest[:n_dom - 1]
    (accel_ref, kicked_ref, ids_ref, lookup_ref, list_ref, reads_ref, wide_ref, acc_ref, sems) = rest[n_dom - 1:]
    me = lax.axis_index("dom")
    loads = [
        pltpu.make_async_copy(source, target, sems.at[n])
        for n, (source, target) in enumerate([
            (list_hbm, list_ref), (ids_hbm, ids_ref), (lookup_hbm, lookup_ref), (reads_hbm, reads_ref),
        ])
    ]
    for load in loads:
        load.start()
    acc_ref[...] = jnp.zeros_like(acc_ref)
    loads[0].wait()

    def two_leaves(k, j):
        pair = [src_refs[k - 1][list_ref[2 * j + u, me ^ k]] for u in range(2)]
        return jnp.concatenate(pair, axis=0)

    spread_tiles(
        [functools.partial(two_leaves, k, j) for k in range(1, n_dom) for j in range(SLOTS // 2)], wide_ref
    )
    for load in loads[1:]:
        load.wait()

    def source_of(i):
        q = ids_ref[1, i]
        return jnp.maximum((q ^ me) - 1, 0) * SLOTS + lookup_ref[q, ids_ref[2, i]]

    def weight_of(i):
        return reads_ref[me, ids_ref[1, i], ids_ref[2, i]].astype(F32)

    pair_loop(ids_ref.shape[1], lambda i: ids_ref[0, i], source_of, weight_of, here_ref, wide_ref, acc_ref)
    leaves = acc_ref.shape[0]
    total = gravity * unpack_sums([local_ref, acc_ref], leaves)
    first = iota((8, LEAF), 0) < 4
    for h in range(leaves // 2):
        rows = slice(8 * h, 8 * h + 8)
        mass = [jnp.broadcast_to(tgt_ref[8 * h + r:8 * h + r + 1, :], (8, LEAF)) for r in (3, 7)]
        accel = jnp.where(jnp.where(first, mass[0], mass[1]) > 0.0, total[rows], 0.0)
        per = vel_ref.shape[1]
        kicked = jnp.concatenate(
            [vel_ref[r // per, r % per:r % per + 4, :] for r in (8 * h, 8 * h + 4)], axis=0
        ) + kick_time * accel
        for u in range(2):
            lanes = slice((2 * h + u) * LEAF, (2 * h + u + 1) * LEAF)
            accel_ref[:, lanes] = accel[4 * u:4 * u + 3]
            kicked_ref[:, lanes] = kicked[4 * u:4 * u + 3]


def remote_forces(near_remote, lookup, lists, reads, near, vel, local, here, arrived):
    n_dom = reads.shape[0]
    rows = near.shape[0]
    leaves = rows // 4
    work = near_remote.shape[1] * LEAF * LEAF
    out = jax.ShapeDtypeStruct((3, leaves * LEAF), F32)
    return pl.pallas_call(
        functools.partial(remote_kernel, n_dom),
        out_shape=(out, out),
        in_specs=[hbm()] * 4 + [vmem()] * (3 + n_dom),
        out_specs=(vmem(), vmem()),
        scratch_shapes=[
            pltpu.SMEM(near_remote.shape, I32),
            pltpu.SMEM(lookup.shape, I32),
            pltpu.SMEM(lists.shape, I32),
            pltpu.SMEM(reads.shape, I32),
            pltpu.VMEM((16, (n_dom - 1) * SLOTS // 2, 8, LEAF), F32),
            pltpu.VMEM((leaves, 4, 8, LEAF), F32),
            pltpu.SemaphoreType.DMA((4,)),
        ],
        compiler_params=params(),
        cost_estimate=pl.CostEstimate(flops=18 * work, transcendentals=work, bytes_accessed=24 * rows * LEAF),
        name="remote_forces",
    )(*in_hbm(near_remote), lookup, lists, *in_hbm(reads), near, vel, local, here, *arrived)


def on_device(positions, masses, velocities, destinations, readers, near_local, near_remote):
    n_sub = lax.axis_size("sub")
    n_dom = lax.axis_size("dom")
    count = positions.shape[1]
    capacity = 5 * count // (4 * n_sub)
    leaves = capacity // LEAF
    reads = readers.reshape(n_dom, n_dom, readers.shape[3])
    near, far, lists, lookup = regroup(positions, masses, velocities, destinations, reads, n_sub, leaves)
    near = lax.all_to_all(near, "sub", split_axis=0, concat_axis=0, tiled=True)
    whole = near.reshape(n_sub * leaves, 4, LEAF)
    arrived = [lax.ppermute(whole, "dom", [(i, i ^ k) for i in range(n_dom)]) for k in range(1, n_dom)]
    far = lax.all_to_all(far, "sub", split_axis=0, concat_axis=0, tiled=True)
    near = near.reshape(n_sub * leaves * 4, LEAF)
    local, here = local_forces(near_local, near)
    return remote_forces(near_remote, lookup, lists, reads, near, far, local, here, arrived)


def solution(mesh):
    in_specs = (
        P(None, ("dom", "sub")),
        P(("dom", "sub")),
        P(None, ("dom", "sub")),
        P(("dom", "sub"), None),
        P(None, None, "sub", None),
        P(None, ("dom", "sub")),
        P(None, ("dom", "sub")),
    )
    out_specs = (P(None, ("dom", "sub")), P(None, ("dom", "sub")))
    return jax.shard_map(
        on_device, mesh=mesh, in_specs=in_specs, out_specs=out_specs, check_vma=False
    )
```

```python
import functools

import jax
import jax.numpy as jnp
from jax import lax
from jax.experimental import pallas as pl
from jax.experimental.pallas import tpu as pltpu
from jax.sharding import PartitionSpec as P

SLOTS = 32
LEAF = 128

softening = 0.01
gravity = 4.0
kick_time = 0.5

VMEM_LIMIT = 48 << 20
F32 = jnp.float32
I32 = jnp.int32
BF16 = jnp.bfloat16


def vmem():
    return pl.BlockSpec(memory_space=pltpu.VMEM)


def smem():
    return pl.BlockSpec(memory_space=pltpu.SMEM)


def hbm():
    return pl.BlockSpec(memory_space=pltpu.HBM)


def in_hbm(*arrays):
    return [pltpu.with_memory_space_constraint(x, pltpu.MemorySpace.HBM) for x in arrays]


def params():
    return pltpu.CompilerParams(vmem_limit_bytes=VMEM_LIMIT)


def lane_gather(tile, index):
    return jnp.take_along_axis(tile, index, axis=1, mode="promise_in_bounds")


def iota(shape, dim):
    return lax.broadcasted_iota(I32, shape, dim)


def as_bf16(condition):
    return jnp.where(condition, 1.0, 0.0).astype(BF16)


def plan_reads(n_dom, reads_ref, ids_ref, local_ref, list_ref, pairs_ref):
    me = lax.axis_index("dom")
    leaves = reads_ref.shape[2]
    pairs = ids_ref.shape[1]
    lower = as_bf16(iota((leaves, leaves), 0) < iota((leaves, leaves), 1))
    wanted = reads_ref[me]
    flags = wanted.astype(F32).astype(BF16)
    place = jnp.minimum(jnp.dot(flags, lower, preferred_element_type=F32), SLOTS - 1.0)
    slot = iota((SLOTS, leaves), 0).astype(F32)
    leaf = iota((SLOTS, leaves), 1)
    lane = iota((SLOTS, LEAF), 1)
    lists = jnp.zeros((SLOTS, LEAF), I32)
    source_dom, source_leaf = ids_ref[1:2, :], ids_ref[2:3, :]
    line = iota((8, leaves), 0)
    looked = jnp.zeros((8, pairs), F32)
    for q in range(n_dom):
        mine = wanted[q:q + 1]
        hit = (place[q:q + 1] == slot) & (mine > 0)
        lists = jnp.where(lane == q, jnp.sum(jnp.where(hit, leaf, 0), axis=1, keepdims=True), lists)
        rows = jnp.where(line == 0, place[q:q + 1], jnp.where(line == 1, mine.astype(F32), 0.0))
        here = as_bf16((iota((leaves, pairs), 0) == source_leaf) & (source_dom == q))
        looked += jnp.dot(rows.astype(BF16), here, preferred_element_type=F32)
    list_ref[...] = lists
    looked = looked.astype(I32)
    pairs_ref[0:1, :] = ids_ref[0:1, :]
    pairs_ref[1:2, :] = jnp.maximum((source_dom ^ me) - 1, 0) * SLOTS + looked[0:1]
    pairs_ref[2:3, :] = looked[1:2]
    pairs_ref[3:5, :] = local_ref[...]
    pairs_ref[5:8, :] = jnp.zeros((3, pairs), I32)


def regroup_kernel(
    n_sub, n_dom, leaves, pos_hbm, mass_hbm, vel_hbm, dest_hbm, reads_hbm, ids_hbm, local_hbm,
    near_ref, far_ref, list_ref, pairs_ref,
    pos_ref, mass_ref, vel_ref, dest_ref, reads_ref, ids_ref, local_ref, tiles, table, ordered,
    off_ref, cnt_ref, start_ref, perm_ref, leaf_vec, leaf_idx, sems
):
    blocks = dest_ref.shape[0]
    loads = [
        pltpu.make_async_copy(source, target, sems.at[n])
        for n, (source, target) in enumerate(
            [(dest_hbm, dest_ref), (reads_hbm, reads_ref), (ids_hbm, ids_ref), (local_hbm, local_ref),
             (pos_hbm, pos_ref), (mass_hbm, mass_ref), (vel_hbm, vel_ref)]
        )
    ]
    for load in loads:
        load.start()
    tiles[...] = jnp.zeros_like(tiles)
    row = iota((LEAF, LEAF), 0)
    weights = jnp.concatenate([as_bf16(row <= iota((LEAF, LEAF), 1)), jnp.ones((LEAF, LEAF), BF16)], axis=1)
    earlier = as_bf16(iota((blocks, blocks), 1) < iota((blocks, blocks), 0))
    lane64 = iota((blocks, LEAF), 1)
    loads[0].wait()
    dest = dest_ref[...]
    masks = [dest == e for e in range(n_sub)]
    ones_of = jnp.concatenate([as_bf16(m) for m in masks], axis=0)
    counts = jnp.dot(ones_of, weights, preferred_element_type=F32)
    start = jnp.zeros((blocks, LEAF), F32)
    place = jnp.zeros((blocks, LEAF), F32)
    leaf_of = jnp.zeros((blocks, LEAF), I32)
    for e in range(n_sub):
        inside = counts[e * blocks:(e + 1) * blocks, :LEAF]
        total = counts[e * blocks:(e + 1) * blocks, LEAF:]
        place = jnp.where(masks[e], inside - 1.0 + start, place)
        offset = jnp.dot(earlier, total.astype(BF16), preferred_element_type=F32).astype(I32)
        count = total.astype(I32)
        off_ref[e] = offset
        cnt_ref[e] = count
        start_ref[e] = start.astype(I32)
        base = e * (leaves + 1)
        leaf_of = jnp.where(lane64 == e, base + (offset >> 7), leaf_of)
        leaf_of = jnp.where(lane64 == n_sub + e, base + ((offset + count) >> 7), leaf_of)
        start = start + total
    leaf_vec[...] = leaf_of
    copy = pltpu.make_async_copy(leaf_vec, leaf_idx, sems.at[7])
    copy.start()
    perm_ref[...] = place.astype(I32)
    for load in loads[1:]:
        load.wait()
    plan_reads(n_dom, reads_ref, ids_ref, local_ref, list_ref, pairs_ref)
    table[:, 7:8, :] = jnp.zeros((blocks, 1, LEAF), F32)
    for b in range(blocks):
        lanes = slice(b * LEAF, (b + 1) * LEAF)
        table[b, 0:3, :] = pos_ref[:, lanes]
        table[b, 3:4, :] = mass_ref[b:b + 1, :]
        table[b, 4:7, :] = vel_ref[:, lanes]
    lane = iota((8, LEAF), 1)
    lane_rows = iota((16, LEAF), 1).astype(F32).astype(BF16)

    def order(b, _):
        onehot = as_bf16(row == perm_ref[pl.ds(b, 1), :])
        inverse = lax.dot_general(
            lane_rows, onehot, (((1,), (1,)), ((), ())), preferred_element_type=F32
        )[:8].astype(I32)
        ordered[b] = lane_gather(table[b], inverse)
        return 0

    lax.fori_loop(0, blocks, order, 0, unroll=32)
    copy.wait()

    def step(b, tails):
        block = ordered[b]
        new = []
        for e in range(n_sub):
            offset = jnp.broadcast_to(off_ref[e, pl.ds(b, 1), :], (8, LEAF))
            count = jnp.broadcast_to(cnt_ref[e, pl.ds(b, 1), :], (8, LEAF))
            first = jnp.broadcast_to(start_ref[e, pl.ds(b, 1), :], (8, LEAF))
            turned = (lane - offset) & (LEAF - 1)
            moved = lane_gather(block, (turned + first) & (LEAF - 1))
            low = offset & (LEAF - 1)
            taken = turned < count
            tail = jnp.where(taken & (lane >= low), moved, tails[e])
            tiles[leaf_idx[b, e]] = tail
            fresh = jnp.where(taken & (lane < low), moved, 0.0)
            new.append(jnp.where(low + count >= LEAF, fresh, tail))
        return tuple(new)

    tails = lax.fori_loop(0, blocks, step, (jnp.zeros((8, LEAF), F32),) * n_sub, unroll=8)
    for e in range(n_sub):
        tiles[leaf_idx[blocks - 1, n_sub + e]] = tails[e]
        for l in range(leaves):
            tile = tiles[e * (leaves + 1) + l]
            near_ref[e, 4 * l:4 * l + 4, :] = tile[0:4]
            far_ref[e, 4 * l:4 * l + 4, :] = tile[4:8]


def regroup(positions, masses, velocities, destinations, reads, near_local, near_remote, n_sub, leaves):
    count = positions.shape[1]
    blocks = count // LEAF
    n_dom = reads.shape[0]
    out = jax.ShapeDtypeStruct((n_sub, leaves * 4, LEAF), F32)
    return pl.pallas_call(
        functools.partial(regroup_kernel, n_sub, n_dom, leaves),
        out_shape=(
            out,
            out,
            jax.ShapeDtypeStruct((SLOTS, LEAF), I32),
            jax.ShapeDtypeStruct((8, near_remote.shape[1]), I32),
        ),
        in_specs=[hbm()] * 7,
        out_specs=(vmem(),) * 4,
        scratch_shapes=[
            pltpu.VMEM((3, count), F32),
            pltpu.VMEM((blocks, LEAF), F32),
            pltpu.VMEM((3, count), F32),
            pltpu.VMEM((blocks, LEAF), I32),
            pltpu.VMEM(reads.shape, I32),
            pltpu.VMEM(near_remote.shape, I32),
            pltpu.VMEM(near_local.shape, I32),
            pltpu.VMEM((n_sub * (leaves + 1), 8, LEAF), F32),
            pltpu.VMEM((blocks, 8, LEAF), F32),
            pltpu.VMEM((blocks, 8, LEAF), F32),
            pltpu.VMEM((n_sub, blocks, LEAF), I32),
            pltpu.VMEM((n_sub, blocks, LEAF), I32),
            pltpu.VMEM((n_sub, blocks, LEAF), I32),
            pltpu.VMEM((blocks, LEAF), I32),
            pltpu.VMEM((blocks, LEAF), I32),
            pltpu.SMEM((blocks, LEAF), I32),
            pltpu.SemaphoreType.DMA((8,)),
        ],
        compiler_params=params(),
        name="regroup",
    )(*in_hbm(
        positions, masses.reshape(blocks, LEAF), velocities, destinations.reshape(blocks, LEAF), reads,
        near_remote, near_local,
    ))


UNROLL = 8


def spread_tiles(tile_of, count, wide_ref):
    group = iota((8, LEAF), 1) & ~15
    for k in range(16):
        for h in range(count):
            wide_ref[k, h] = lane_gather(tile_of(h), group + k)


def live_pairs(targets, sources, flags, target_mass, source_mass, list_ref):
    pairs = targets.shape[1]
    spare = target_mass.shape[0]

    def filled(ids, mass):
        some = jnp.broadcast_to(mass[:, :1] > 0.0, (mass.shape[0], pairs))
        pick = as_bf16((iota((mass.shape[0], pairs), 0) == ids) & some)
        return jnp.dot(jnp.ones((8, mass.shape[0]), BF16), pick, preferred_element_type=F32)

    live = filled(targets, target_mass) * filled(sources, source_mass)
    if flags is not None:
        live = live * flags.astype(F32)
    row, col = iota((pairs, pairs), 0), iota((pairs, pairs), 1)
    place = jnp.dot(live.astype(BF16), as_bf16(row < col), preferred_element_type=F32).astype(I32)
    move = as_bf16((place[:1] == row) & (live[:1] > 0.0))
    line = iota((8, pairs), 0)
    rows = jnp.where(line == 0, targets.astype(F32), jnp.where(line == 1, sources.astype(F32), 1.0))
    moved = lax.dot_general(
        rows.astype(BF16), move, (((1,), (1,)), ((), ())), preferred_element_type=F32
    ).astype(I32)
    count = jnp.sum(live, axis=1, keepdims=True).astype(I32)
    moved = jnp.where((line == 0) & (moved[2:3] == 0), spare, moved)
    list_ref[...] = jnp.where(line == 2, count, moved)


def pair_loop(list_ref, here_ref, wide_ref, acc_ref):
    def pair(i):
        t = list_ref[0, i]
        s = list_ref[1, i]
        h, first = s >> 1, (s & 1) * 4
        here = [here_ref[t, c] for c in range(3)]
        sums = None
        for k in range(16):
            there = [jnp.broadcast_to(wide_ref[k, h, pl.ds(first + c, 1), :], (8, LEAF)) for c in range(4)]
            delta = [there[c] - here[c] for c in range(3)]
            dist = delta[0] * delta[0] + delta[1] * delta[1] + (delta[2] * delta[2] + softening)
            inv = lax.rsqrt(dist)
            weight = (there[3] * inv) * (inv * inv)
            terms = [weight * delta[c] for c in range(3)]
            sums = terms if sums is None else [sums[c] + terms[c] for c in range(3)]
        for c in range(3):
            acc_ref[t, c] += sums[c]

    def step(j, _):
        for u in range(UNROLL):
            pair(j * UNROLL + u)
        return 0

    lax.fori_loop(0, (list_ref[2, 0] + UNROLL - 1) // UNROLL, step, 0)


def local_kernel(ids_ref, src_ref, acc_ref, here_ref, wide_ref, list_vec, list_ref, sem):
    leaves = acc_ref.shape[0] - 1
    mass = src_ref[pl.ds(3, leaves, stride=4), :]
    live_pairs(ids_ref[3:4, :], ids_ref[4:5, :], None, mass, mass, list_vec)
    copy = pltpu.make_async_copy(list_vec, list_ref, sem)
    copy.start()
    spread_tiles(lambda h: src_ref[8 * h:8 * h + 8, :], leaves // 2, wide_ref)
    fold = iota((8, LEAF), 0) * 16 + (iota((8, LEAF), 1) & 15)
    for t in range(leaves):
        for c in range(3):
            line = src_ref[4 * t + c:4 * t + c + 1, :]
            here_ref[t, c] = lane_gather(jnp.broadcast_to(line, (8, LEAF)), fold)
    here_ref[leaves] = jnp.zeros((3, 8, LEAF), F32)
    acc_ref[...] = jnp.zeros_like(acc_ref)
    copy.wait()
    pair_loop(list_ref, here_ref, wide_ref, acc_ref)


def local_forces(ids, near):
    rows = near.shape[0]
    leaves = rows // 4
    pairs = ids.shape[1]
    assert pairs % UNROLL == 0
    work = pairs * LEAF * LEAF
    return pl.pallas_call(
        local_kernel,
        out_shape=(
            jax.ShapeDtypeStruct((leaves + 1, 4, 8, LEAF), F32),
            jax.ShapeDtypeStruct((leaves + 1, 3, 8, LEAF), F32),
        ),
        in_specs=[vmem(), vmem()],
        out_specs=(vmem(), vmem()),
        scratch_shapes=[
            pltpu.VMEM((16, rows // 8, 8, LEAF), F32),
            pltpu.VMEM((8, pairs), I32),
            pltpu.SMEM((8, pairs), I32),
            pltpu.SemaphoreType.DMA,
        ],
        compiler_params=params(),
        cost_estimate=pl.CostEstimate(flops=18 * work, transcendentals=work, bytes_accessed=8 * rows * LEAF),
        name="local_forces",
    )(ids, near)


def three_parts(x):
    high = x.astype(BF16)
    rest = x - high.astype(F32)
    middle = rest.astype(BF16)
    return [high, middle, (rest - middle.astype(F32)).astype(BF16)]


def unpack_sums(acc_refs, leaves):
    source, target = iota((LEAF, LEAF), 0), iota((LEAF, LEAF), 1)
    parts, picks = [], []
    for s in range(8):
        lines = [ref.reshape((leaves + 1) * 32, LEAF)[pl.ds(s, leaves * 4, stride=8), :] for ref in acc_refs]
        pick = as_bf16(((source & 15) == (target & 15)) & ((target >> 4) == s))
        parts += three_parts(sum(lines[1:], lines[0]))
        picks += [pick] * 3
    return jnp.dot(
        jnp.concatenate(parts, axis=1), jnp.concatenate(picks, axis=0), preferred_element_type=F32
    )


def remote_kernel(n_dom, leaf_list, pairs_ref, tgt_ref, vel_ref, local_ref, here_ref, *rest):
    src_refs = rest[:n_dom - 1]
    (accel_ref, kicked_ref, leaf_ref, chosen_ref, wide_ref, acc_ref, list_vec, list_ref,
     sems) = rest[n_dom - 1:]
    me = lax.axis_index("dom")
    load = pltpu.make_async_copy(leaf_list, leaf_ref, sems.at[0])
    load.start()
    leaves = acc_ref.shape[0] - 1
    acc_ref[...] = jnp.zeros_like(acc_ref)
    slots = (n_dom - 1) * SLOTS
    load.wait()
    for k in range(1, n_dom):
        for j in range(SLOTS):
            at = 4 * ((k - 1) * SLOTS + j)
            chosen_ref[at:at + 4, :] = src_refs[k - 1][leaf_ref[j, me ^ k]]
    live_pairs(
        pairs_ref[0:1, :], pairs_ref[1:2, :], pairs_ref[2:3, :],
        tgt_ref[pl.ds(3, leaves, stride=4), :], chosen_ref[pl.ds(3, slots, stride=4), :], list_vec,
    )
    copy = pltpu.make_async_copy(list_vec, list_ref, sems.at[1])
    copy.start()
    spread_tiles(lambda h: chosen_ref[8 * h:8 * h + 8, :], slots // 2, wide_ref)
    copy.wait()
    pair_loop(list_ref, here_ref, wide_ref, acc_ref)
    total = gravity * unpack_sums([local_ref, acc_ref], leaves)
    first = iota((8, LEAF), 0) < 4
    per = vel_ref.shape[1]
    for h in range(leaves // 2):
        rows = slice(8 * h, 8 * h + 8)
        mass = [jnp.broadcast_to(tgt_ref[8 * h + r:8 * h + r + 1, :], (8, LEAF)) for r in (3, 7)]
        accel = jnp.where(jnp.where(first, mass[0], mass[1]) > 0.0, total[rows], 0.0)
        kicked = jnp.concatenate(
            [vel_ref[r // per, r % per:r % per + 4, :] for r in (8 * h, 8 * h + 4)], axis=0
        ) + kick_time * accel
        for u in range(2):
            lanes = slice((2 * h + u) * LEAF, (2 * h + u + 1) * LEAF)
            accel_ref[:, lanes] = accel[4 * u:4 * u + 3]
            kicked_ref[:, lanes] = kicked[4 * u:4 * u + 3]


def remote_forces(lists, pairs, near, vel, local, here, arrived):
    n_dom = len(arrived) + 1
    rows = near.shape[0]
    leaves = rows // 4
    slots = (n_dom - 1) * SLOTS
    work = pairs.shape[1] * LEAF * LEAF
    assert pairs.shape[1] % UNROLL == 0
    out = jax.ShapeDtypeStruct((3, leaves * LEAF), F32)
    return pl.pallas_call(
        functools.partial(remote_kernel, n_dom),
        out_shape=(out, out),
        in_specs=[vmem()] * (5 + n_dom),
        out_specs=(vmem(), vmem()),
        scratch_shapes=[
            pltpu.SMEM(lists.shape, I32),
            pltpu.VMEM((slots * 4, LEAF), F32),
            pltpu.VMEM((16, slots // 2, 8, LEAF), F32),
            pltpu.VMEM((leaves + 1, 4, 8, LEAF), F32),
            pltpu.VMEM(pairs.shape, I32),
            pltpu.SMEM(pairs.shape, I32),
            pltpu.SemaphoreType.DMA((2,)),
        ],
        compiler_params=params(),
        cost_estimate=pl.CostEstimate(flops=18 * work, transcendentals=work, bytes_accessed=24 * rows * LEAF),
        name="remote_forces",
    )(lists, pairs, near, vel, local, here, *arrived)


def on_device(positions, masses, velocities, destinations, readers, near_local, near_remote):
    n_sub = lax.axis_size("sub")
    n_dom = lax.axis_size("dom")
    count = positions.shape[1]
    capacity = 5 * count // (4 * n_sub)
    leaves = capacity // LEAF
    reads = readers.reshape(n_dom, n_dom, readers.shape[3])
    near, far, lists, pairs = regroup(
        positions, masses, velocities, destinations, reads, near_local, near_remote, n_sub, leaves
    )
    near = lax.all_to_all(near, "sub", split_axis=0, concat_axis=0, tiled=True)
    whole = near.reshape(n_sub * leaves, 4, LEAF)
    arrived = [lax.ppermute(whole, "dom", [(i, i ^ k) for i in range(n_dom)]) for k in range(1, n_dom)]
    far = lax.all_to_all(far, "sub", split_axis=0, concat_axis=0, tiled=True)
    near = near.reshape(n_sub * leaves * 4, LEAF)
    local, here = local_forces(pairs, near)
    return remote_forces(lists, pairs, near, far, local, here, arrived)


def solution(mesh):
    in_specs = (
        P(None, ("dom", "sub")),
        P(("dom", "sub")),
        P(None, ("dom", "sub")),
        P(("dom", "sub"), None),
        P(None, None, "sub", None),
        P(None, ("dom", "sub")),
        P(None, ("dom", "sub")),
    )
    out_specs = (P(None, ("dom", "sub")), P(None, ("dom", "sub")))
    return jax.shard_map(
        on_device, mesh=mesh, in_specs=in_specs, out_specs=out_specs, check_vma=False
    )
```

```python
import functools

import jax
import jax.numpy as jnp
from jax import lax
from jax.experimental import pallas as pl
from jax.experimental.pallas import tpu as pltpu
from jax.sharding import PartitionSpec as P

SLOTS = 32
LEAF = 128

softening = 0.01
gravity = 4.0
kick_time = 0.5

VMEM_LIMIT = 48 << 20
F32 = jnp.float32
I32 = jnp.int32
BF16 = jnp.bfloat16


def vmem():
    return pl.BlockSpec(memory_space=pltpu.VMEM)


def smem():
    return pl.BlockSpec(memory_space=pltpu.SMEM)


def hbm():
    return pl.BlockSpec(memory_space=pltpu.HBM)


def in_hbm(*arrays):
    return [pltpu.with_memory_space_constraint(x, pltpu.MemorySpace.HBM) for x in arrays]


def params():
    return pltpu.CompilerParams(vmem_limit_bytes=VMEM_LIMIT)


def lane_gather(tile, index):
    return jnp.take_along_axis(tile, index, axis=1, mode="promise_in_bounds")


def iota(shape, dim):
    return lax.broadcasted_iota(I32, shape, dim)


def as_bf16(condition):
    return jnp.where(condition, 1.0, 0.0).astype(BF16)


def plan_reads(n_dom, reads_ref, ids_ref, local_ref, list_ref, pairs_ref):
    me = lax.axis_index("dom")
    leaves = reads_ref.shape[2]
    pairs = ids_ref.shape[1]
    lower = as_bf16(iota((leaves, leaves), 0) < iota((leaves, leaves), 1))
    wanted = reads_ref[me]
    flags = wanted.astype(F32).astype(BF16)
    place = jnp.minimum(jnp.dot(flags, lower, preferred_element_type=F32), SLOTS - 1.0)
    slot = iota((SLOTS, leaves), 0).astype(F32)
    leaf = iota((SLOTS, leaves), 1)
    lane = iota((SLOTS, LEAF), 1)
    lists = jnp.zeros((SLOTS, LEAF), I32)
    source_dom, source_leaf = ids_ref[1:2, :], ids_ref[2:3, :]
    line = iota((8, leaves), 0)
    looked = jnp.zeros((8, pairs), F32)
    for q in range(n_dom):
        mine = wanted[q:q + 1]
        hit = (place[q:q + 1] == slot) & (mine > 0)
        lists = jnp.where(lane == q, jnp.sum(jnp.where(hit, leaf, 0), axis=1, keepdims=True), lists)
        rows = jnp.where(line == 0, place[q:q + 1], jnp.where(line == 1, mine.astype(F32), 0.0))
        here = as_bf16((iota((leaves, pairs), 0) == source_leaf) & (source_dom == q))
        looked += jnp.dot(rows.astype(BF16), here, preferred_element_type=F32)
    list_ref[...] = lists
    looked = looked.astype(I32)
    pairs_ref[0:1, :] = ids_ref[0:1, :]
    pairs_ref[1:2, :] = jnp.maximum((source_dom ^ me) - 1, 0) * SLOTS + looked[0:1]
    pairs_ref[2:3, :] = looked[1:2]
    pairs_ref[3:5, :] = local_ref[...]
    pairs_ref[5:8, :] = jnp.zeros((3, pairs), I32)


def start_copies(sems, *pairs):
    loads = [pltpu.make_async_copy(source, target, sems.at[n]) for n, (source, target) in enumerate(pairs)]
    for load in loads:
        load.start()
    return loads


def by_half(ref, b, half):
    rows = [jnp.broadcast_to(ref[pl.ds(b + at, 1), :], (8, LEAF)) for at in (0, half)]
    return jnp.where(iota((8, LEAF), 0) < 4, rows[0], rows[1])


def place_particles(n_sub, leaves, ordered, spans, leaf_idx, tiles, out_ref):
    off_ref, cnt_ref, start_ref = spans
    half = ordered.shape[0]
    lane = iota((8, LEAF), 1)

    def step(b, tails):
        block = ordered[b]
        new = []
        for e in range(n_sub):
            offset = by_half(off_ref.at[e], b, half)
            count = by_half(cnt_ref.at[e], b, half)
            first = by_half(start_ref.at[e], b, half)
            turned = (lane - offset) & (LEAF - 1)
            moved = lane_gather(block, (turned + first) & (LEAF - 1))
            low = offset & (LEAF - 1)
            taken = turned < count
            tail = jnp.where(taken & (lane >= low), moved, tails[e])
            tiles[leaf_idx[b, e], 0:4, :] = tail[0:4]
            tiles[leaf_idx[b + half, e], 4:8, :] = tail[4:8]
            fresh = jnp.where(taken & (lane < low), moved, 0.0)
            new.append(jnp.where(low + count >= LEAF, fresh, tail))
        return tuple(new)

    tails = lax.fori_loop(0, half, step, (jnp.zeros((8, LEAF), F32),) * n_sub, unroll=8)
    for e in range(n_sub):
        tiles[leaf_idx[half - 1, n_sub + e], 0:4, :] = tails[e][0:4]
        tiles[leaf_idx[2 * half - 1, n_sub + e], 4:8, :] = tails[e][4:8]
        for l in range(leaves):
            tile = tiles[e * (leaves + 1) + l]
            out_ref[e, 4 * l:4 * l + 4, :] = tile[0:4] + tile[4:8]


def regroup_kernel(
    n_sub, leaves, pos_hbm, mass_hbm, dest_hbm, near_ref, off_ref, cnt_ref, start_ref, inv_ref, leaf_vec,
    pos_ref, mass_ref, dest_ref, tiles, table, ordered, perm_ref, leaf_idx, sems
):
    blocks = dest_ref.shape[0]
    half = blocks // 2
    loads = start_copies(sems, (dest_hbm, dest_ref), (pos_hbm, pos_ref), (mass_hbm, mass_ref))
    tiles[...] = jnp.zeros_like(tiles)
    row = iota((LEAF, LEAF), 0)
    weights = jnp.concatenate([as_bf16(row <= iota((LEAF, LEAF), 1)), jnp.ones((LEAF, LEAF), BF16)], axis=1)
    earlier = as_bf16(iota((blocks, blocks), 1) < iota((blocks, blocks), 0))
    lane64 = iota((blocks, LEAF), 1)
    loads[0].wait()
    dest = dest_ref[...]
    masks = [dest == e for e in range(n_sub)]
    ones_of = jnp.concatenate([as_bf16(m) for m in masks], axis=0)
    counts = jnp.dot(ones_of, weights, preferred_element_type=F32)
    start = jnp.zeros((blocks, LEAF), F32)
    place = jnp.zeros((blocks, LEAF), F32)
    leaf_of = jnp.zeros((blocks, LEAF), I32)
    for e in range(n_sub):
        inside = counts[e * blocks:(e + 1) * blocks, :LEAF]
        total = counts[e * blocks:(e + 1) * blocks, LEAF:]
        place = jnp.where(masks[e], inside - 1.0 + start, place)
        offset = jnp.dot(earlier, total.astype(BF16), preferred_element_type=F32).astype(I32)
        count = total.astype(I32)
        off_ref[e] = offset
        cnt_ref[e] = count
        start_ref[e] = start.astype(I32)
        base = e * (leaves + 1)
        leaf_of = jnp.where(lane64 == e, base + (offset >> 7), leaf_of)
        leaf_of = jnp.where(lane64 == n_sub + e, base + ((offset + count) >> 7), leaf_of)
        start = start + total
    leaf_vec[...] = leaf_of
    copy = pltpu.make_async_copy(leaf_vec, leaf_idx, sems.at[3])
    copy.start()
    perm_ref[...] = place.astype(I32)
    for load in loads[1:]:
        load.wait()
    for b in range(blocks):
        at = b // half * 4
        table[b % half, at:at + 3, :] = pos_ref[:, b * LEAF:(b + 1) * LEAF]
        table[b % half, at + 3:at + 4, :] = mass_ref[b:b + 1, :]
    lane_rows = iota((16, LEAF), 1).astype(F32).astype(BF16)
    upper_half = iota((8, LEAF), 0) < 4

    def order(b, _):
        inverse = []
        for at in (b, b + half):
            onehot = as_bf16(row == perm_ref[pl.ds(at, 1), :])
            found = lax.dot_general(
                lane_rows, onehot, (((1,), (1,)), ((), ())), preferred_element_type=F32
            )[:8].astype(I32)
            inv_ref[pl.ds(at, 1), :] = found[:1]
            inverse.append(found)
        ordered[b] = lane_gather(table[b], jnp.where(upper_half, inverse[0], inverse[1]))
        return 0

    lax.fori_loop(0, half, order, 0, unroll=16)
    copy.wait()
    place_particles(n_sub, leaves, ordered, (off_ref, cnt_ref, start_ref), leaf_idx, tiles, near_ref)


def regroup(positions, masses, destinations, n_sub, leaves):
    count = positions.shape[1]
    blocks = count // LEAF
    spans = jax.ShapeDtypeStruct((n_sub, blocks, LEAF), I32)
    rows = jax.ShapeDtypeStruct((blocks, LEAF), I32)
    return pl.pallas_call(
        functools.partial(regroup_kernel, n_sub, leaves),
        out_shape=(jax.ShapeDtypeStruct((n_sub, leaves * 4, LEAF), F32), spans, spans, spans, rows, rows),
        in_specs=[hbm()] * 3,
        out_specs=(vmem(),) * 6,
        scratch_shapes=[
            pltpu.VMEM((3, count), F32),
            pltpu.VMEM((blocks, LEAF), F32),
            pltpu.VMEM((blocks, LEAF), I32),
            pltpu.VMEM((n_sub * (leaves + 1), 8, LEAF), F32),
            pltpu.VMEM((blocks // 2, 8, LEAF), F32),
            pltpu.VMEM((blocks // 2, 8, LEAF), F32),
            pltpu.VMEM((blocks, LEAF), I32),
            pltpu.SMEM((blocks, LEAF), I32),
            pltpu.SemaphoreType.DMA((4,)),
        ],
        compiler_params=params(),
        name="regroup",
    )(*in_hbm(positions, masses.reshape(blocks, LEAF), destinations.reshape(blocks, LEAF)))


def velocity_kernel(
    n_sub, n_dom, leaves, vel_hbm, reads_hbm, ids_hbm, local_hbm, off_ref, cnt_ref, start_ref, inv_ref, leaf_vec,
    far_ref, list_ref, pairs_ref, vel_ref, reads_ref, ids_ref, local_ref, tiles, table, ordered, leaf_idx, sems
):
    half = ordered.shape[0]
    loads = start_copies(
        sems, (vel_hbm, vel_ref), (leaf_vec, leaf_idx), (reads_hbm, reads_ref), (ids_hbm, ids_ref),
        (local_hbm, local_ref),
    )
    tiles[...] = jnp.zeros_like(tiles)
    table[...] = jnp.zeros_like(table)
    for load in loads:
        load.wait()
    plan_reads(n_dom, reads_ref, ids_ref, local_ref, list_ref, pairs_ref)
    for b in range(2 * half):
        at = b // half * 4
        table[b % half, at:at + 3, :] = vel_ref[:, b * LEAF:(b + 1) * LEAF]

    def order(b, _):
        ordered[b] = lane_gather(table[b], by_half(inv_ref, b, half))
        return 0

    lax.fori_loop(0, half, order, 0, unroll=8)
    place_particles(n_sub, leaves, ordered, (off_ref, cnt_ref, start_ref), leaf_idx, tiles, far_ref)


def regroup_velocities(velocities, reads, near_local, near_remote, tables, n_sub, leaves):
    count = velocities.shape[1]
    blocks = count // LEAF
    n_dom = reads.shape[0]
    return pl.pallas_call(
        functools.partial(velocity_kernel, n_sub, n_dom, leaves),
        out_shape=(
            jax.ShapeDtypeStruct((n_sub, leaves * 4, LEAF), F32),
            jax.ShapeDtypeStruct((SLOTS, LEAF), I32),
            jax.ShapeDtypeStruct((8, near_remote.shape[1]), I32),
        ),
        in_specs=[hbm()] * 4 + [vmem()] * 5,
        out_specs=(vmem(),) * 3,
        scratch_shapes=[
            pltpu.VMEM((3, count), F32),
            pltpu.VMEM(reads.shape, I32),
            pltpu.VMEM(near_remote.shape, I32),
            pltpu.VMEM(near_local.shape, I32),
            pltpu.VMEM((n_sub * (leaves + 1), 8, LEAF), F32),
            pltpu.VMEM((blocks // 2, 8, LEAF), F32),
            pltpu.VMEM((blocks // 2, 8, LEAF), F32),
            pltpu.SMEM((blocks, LEAF), I32),
            pltpu.SemaphoreType.DMA((5,)),
        ],
        compiler_params=params(),
        cost_estimate=pl.CostEstimate(flops=200 * n_sub * count, transcendentals=0, bytes_accessed=400 * count),
        name="regroup_velocities",
    )(*in_hbm(velocities, reads, near_remote, near_local), *tables)


UNROLL = 8


def spread_tiles(tile_of, count, wide_ref):
    group = iota((8, LEAF), 1) & ~15
    for k in range(16):
        for h in range(count):
            wide_ref[k, h] = lane_gather(tile_of(h), group + k)


def live_pairs(targets, sources, flags, target_mass, source_mass, list_ref):
    pairs = targets.shape[1]
    spare = target_mass.shape[0]

    def filled(ids, mass):
        some = jnp.broadcast_to(mass[:, :1] > 0.0, (mass.shape[0], pairs))
        pick = as_bf16((iota((mass.shape[0], pairs), 0) == ids) & some)
        return jnp.dot(jnp.ones((8, mass.shape[0]), BF16), pick, preferred_element_type=F32)

    live = filled(targets, target_mass) * filled(sources, source_mass)
    if flags is not None:
        live = live * flags.astype(F32)
    row, col = iota((pairs, pairs), 0), iota((pairs, pairs), 1)
    place = jnp.dot(live.astype(BF16), as_bf16(row < col), preferred_element_type=F32).astype(I32)
    move = as_bf16((place[:1] == row) & (live[:1] > 0.0))
    line = iota((8, pairs), 0)
    rows = jnp.where(line == 0, targets.astype(F32), jnp.where(line == 1, sources.astype(F32), 1.0))
    moved = lax.dot_general(
        rows.astype(BF16), move, (((1,), (1,)), ((), ())), preferred_element_type=F32
    ).astype(I32)
    count = jnp.sum(live, axis=1, keepdims=True).astype(I32)
    moved = jnp.where((line == 0) & (moved[2:3] == 0), spare, moved)
    list_ref[...] = jnp.where(line == 2, count, moved)


def pair_loop(list_ref, here_ref, wide_ref, acc_ref):
    def pair(i):
        t = list_ref[0, i]
        s = list_ref[1, i]
        h, first = s >> 1, (s & 1) * 4
        here = [here_ref[t, c] for c in range(3)]
        sums = None
        for k in range(16):
            there = [jnp.broadcast_to(wide_ref[k, h, pl.ds(first + c, 1), :], (8, LEAF)) for c in range(4)]
            delta = [there[c] - here[c] for c in range(3)]
            dist = delta[0] * delta[0] + delta[1] * delta[1] + (delta[2] * delta[2] + softening)
            inv = lax.rsqrt(dist)
            weight = (there[3] * inv) * (inv * inv)
            terms = [weight * delta[c] for c in range(3)]
            sums = terms if sums is None else [sums[c] + terms[c] for c in range(3)]
        for c in range(3):
            acc_ref[t, c] += sums[c]

    def step(j, _):
        for u in range(UNROLL):
            pair(j * UNROLL + u)
        return 0

    lax.fori_loop(0, (list_ref[2, 0] + UNROLL - 1) // UNROLL, step, 0)


def local_kernel(ids_ref, src_ref, acc_ref, here_ref, wide_ref, list_vec, list_ref, sem):
    leaves = acc_ref.shape[0] - 1
    mass = src_ref[pl.ds(3, leaves, stride=4), :]
    live_pairs(ids_ref[3:4, :], ids_ref[4:5, :], None, mass, mass, list_vec)
    copy = pltpu.make_async_copy(list_vec, list_ref, sem)
    copy.start()
    spread_tiles(lambda h: src_ref[8 * h:8 * h + 8, :], leaves // 2, wide_ref)
    fold = iota((8, LEAF), 0) * 16 + (iota((8, LEAF), 1) & 15)
    for t in range(leaves):
        for c in range(3):
            line = src_ref[4 * t + c:4 * t + c + 1, :]
            here_ref[t, c] = lane_gather(jnp.broadcast_to(line, (8, LEAF)), fold)
    here_ref[leaves] = jnp.zeros((3, 8, LEAF), F32)
    acc_ref[...] = jnp.zeros_like(acc_ref)
    copy.wait()
    pair_loop(list_ref, here_ref, wide_ref, acc_ref)


def local_forces(ids, near):
    rows = near.shape[0]
    leaves = rows // 4
    pairs = ids.shape[1]
    assert pairs % UNROLL == 0
    work = pairs * LEAF * LEAF
    return pl.pallas_call(
        local_kernel,
        out_shape=(
            jax.ShapeDtypeStruct((leaves + 1, 4, 8, LEAF), F32),
            jax.ShapeDtypeStruct((leaves + 1, 3, 8, LEAF), F32),
        ),
        in_specs=[vmem(), vmem()],
        out_specs=(vmem(), vmem()),
        scratch_shapes=[
            pltpu.VMEM((16, rows // 8, 8, LEAF), F32),
            pltpu.VMEM((8, pairs), I32),
            pltpu.SMEM((8, pairs), I32),
            pltpu.SemaphoreType.DMA,
        ],
        compiler_params=params(),
        cost_estimate=pl.CostEstimate(flops=18 * work, transcendentals=work, bytes_accessed=8 * rows * LEAF),
        name="local_forces",
    )(ids, near)


def three_parts(x):
    high = x.astype(BF16)
    rest = x - high.astype(F32)
    middle = rest.astype(BF16)
    return [high, middle, (rest - middle.astype(F32)).astype(BF16)]


def unpack_sums(acc_refs, leaves):
    source, target = iota((LEAF, LEAF), 0), iota((LEAF, LEAF), 1)
    parts, picks = [], []
    for s in range(8):
        lines = [ref.reshape((leaves + 1) * 32, LEAF)[pl.ds(s, leaves * 4, stride=8), :] for ref in acc_refs]
        pick = as_bf16(((source & 15) == (target & 15)) & ((target >> 4) == s))
        parts += three_parts(sum(lines[1:], lines[0]))
        picks += [pick] * 3
    return jnp.dot(
        jnp.concatenate(parts, axis=1), jnp.concatenate(picks, axis=0), preferred_element_type=F32
    )


def remote_kernel(n_dom, leaf_list, pairs_ref, tgt_ref, vel_ref, local_ref, here_ref, *rest):
    src_refs = rest[:n_dom - 1]
    (accel_ref, kicked_ref, leaf_ref, chosen_ref, wide_ref, acc_ref, list_vec, list_ref,
     sems) = rest[n_dom - 1:]
    me = lax.axis_index("dom")
    load = pltpu.make_async_copy(leaf_list, leaf_ref, sems.at[0])
    load.start()
    leaves = acc_ref.shape[0] - 1
    acc_ref[...] = jnp.zeros_like(acc_ref)
    slots = (n_dom - 1) * SLOTS
    load.wait()
    for k in range(1, n_dom):
        for j in range(SLOTS):
            at = 4 * ((k - 1) * SLOTS + j)
            chosen_ref[at:at + 4, :] = src_refs[k - 1][leaf_ref[j, me ^ k]]
    live_pairs(
        pairs_ref[0:1, :], pairs_ref[1:2, :], pairs_ref[2:3, :],
        tgt_ref[pl.ds(3, leaves, stride=4), :], chosen_ref[pl.ds(3, slots, stride=4), :], list_vec,
    )
    copy = pltpu.make_async_copy(list_vec, list_ref, sems.at[1])
    copy.start()
    spread_tiles(lambda h: chosen_ref[8 * h:8 * h + 8, :], slots // 2, wide_ref)
    copy.wait()
    pair_loop(list_ref, here_ref, wide_ref, acc_ref)
    total = gravity * unpack_sums([local_ref, acc_ref], leaves)
    first = iota((8, LEAF), 0) < 4
    per = vel_ref.shape[1]
    for h in range(leaves // 2):
        rows = slice(8 * h, 8 * h + 8)
        mass = [jnp.broadcast_to(tgt_ref[8 * h + r:8 * h + r + 1, :], (8, LEAF)) for r in (3, 7)]
        accel = jnp.where(jnp.where(first, mass[0], mass[1]) > 0.0, total[rows], 0.0)
        kicked = jnp.concatenate(
            [vel_ref[r // per, r % per:r % per + 4, :] for r in (8 * h, 8 * h + 4)], axis=0
        ) + kick_time * accel
        for u in range(2):
            lanes = slice((2 * h + u) * LEAF, (2 * h + u + 1) * LEAF)
            accel_ref[:, lanes] = accel[4 * u:4 * u + 3]
            kicked_ref[:, lanes] = kicked[4 * u:4 * u + 3]


def remote_forces(lists, pairs, near, vel, local, here, arrived):
    n_dom = len(arrived) + 1
    rows = near.shape[0]
    leaves = rows // 4
    slots = (n_dom - 1) * SLOTS
    work = pairs.shape[1] * LEAF * LEAF
    assert pairs.shape[1] % UNROLL == 0
    out = jax.ShapeDtypeStruct((3, leaves * LEAF), F32)
    return pl.pallas_call(
        functools.partial(remote_kernel, n_dom),
        out_shape=(out, out),
        in_specs=[vmem()] * (5 + n_dom),
        out_specs=(vmem(), vmem()),
        scratch_shapes=[
            pltpu.SMEM(lists.shape, I32),
            pltpu.VMEM((slots * 4, LEAF), F32),
            pltpu.VMEM((16, slots // 2, 8, LEAF), F32),
            pltpu.VMEM((leaves + 1, 4, 8, LEAF), F32),
            pltpu.VMEM(pairs.shape, I32),
            pltpu.SMEM(pairs.shape, I32),
            pltpu.SemaphoreType.DMA((2,)),
        ],
        compiler_params=params(),
        cost_estimate=pl.CostEstimate(flops=18 * work, transcendentals=work, bytes_accessed=24 * rows * LEAF),
        name="remote_forces",
    )(lists, pairs, near, vel, local, here, *arrived)


def on_device(positions, masses, velocities, destinations, readers, near_local, near_remote):
    n_sub = lax.axis_size("sub")
    n_dom = lax.axis_size("dom")
    count = positions.shape[1]
    capacity = 5 * count // (4 * n_sub)
    leaves = capacity // LEAF
    reads = readers.reshape(n_dom, n_dom, readers.shape[3])
    near, *tables = regroup(positions, masses, destinations, n_sub, leaves)
    near = lax.all_to_all(near, "sub", split_axis=0, concat_axis=0, tiled=True)
    far, lists, pairs = regroup_velocities(velocities, reads, near_local, near_remote, tables, n_sub, leaves)
    near, far, lists, pairs = lax.optimization_barrier((near, far, lists, pairs))
    whole = near.reshape(n_sub * leaves, 4, LEAF)
    arrived = [lax.ppermute(whole, "dom", [(i, i ^ k) for i in range(n_dom)]) for k in range(1, n_dom)]
    far = lax.all_to_all(far, "sub", split_axis=0, concat_axis=0, tiled=True)
    near = near.reshape(n_sub * leaves * 4, LEAF)
    local, here = local_forces(pairs, near)
    return remote_forces(lists, pairs, near, far, local, here, arrived)


def solution(mesh):
    in_specs = (
        P(None, ("dom", "sub")),
        P(("dom", "sub")),
        P(None, ("dom", "sub")),
        P(("dom", "sub"), None),
        P(None, None, "sub", None),
        P(None, ("dom", "sub")),
        P(None, ("dom", "sub")),
    )
    out_specs = (P(None, ("dom", "sub")), P(None, ("dom", "sub")))
    return jax.shard_map(
        on_device, mesh=mesh, in_specs=in_specs, out_specs=out_specs, check_vma=False
    )
```

```python
import functools

import jax
import jax.numpy as jnp
from jax import lax
from jax.experimental import pallas as pl
from jax.experimental.pallas import tpu as pltpu
from jax.sharding import PartitionSpec as P

SLOTS = 32
LEAF = 128

softening = 0.01
gravity = 4.0
kick_time = 0.5

VMEM_LIMIT = 48 << 20
F32 = jnp.float32
I32 = jnp.int32
BF16 = jnp.bfloat16


def vmem():
    return pl.BlockSpec(memory_space=pltpu.VMEM)


def smem():
    return pl.BlockSpec(memory_space=pltpu.SMEM)


def hbm():
    return pl.BlockSpec(memory_space=pltpu.HBM)


def in_hbm(*arrays):
    return [pltpu.with_memory_space_constraint(x, pltpu.MemorySpace.HBM) for x in arrays]


def params():
    return pltpu.CompilerParams(vmem_limit_bytes=VMEM_LIMIT)


def lane_gather(tile, index):
    return jnp.take_along_axis(tile, index, axis=1, mode="promise_in_bounds")


def iota(shape, dim):
    return lax.broadcasted_iota(I32, shape, dim)


def as_bf16(condition):
    return jnp.where(condition, 1.0, 0.0).astype(BF16)


def plan_reads(n_dom, reads_ref, ids_ref, local_ref, list_ref, pairs_ref):
    me = lax.axis_index("dom")
    leaves = reads_ref.shape[2]
    pairs = ids_ref.shape[1]
    lower = as_bf16(iota((leaves, leaves), 0) < iota((leaves, leaves), 1))
    wanted = reads_ref[me]
    flags = wanted.astype(F32).astype(BF16)
    place = jnp.minimum(jnp.dot(flags, lower, preferred_element_type=F32), SLOTS - 1.0)
    slot = iota((SLOTS, leaves), 0).astype(F32)
    leaf = iota((SLOTS, leaves), 1)
    lane = iota((SLOTS, LEAF), 1)
    lists = jnp.zeros((SLOTS, LEAF), I32)
    source_dom, source_leaf = ids_ref[1:2, :], ids_ref[2:3, :]
    line = iota((8, leaves), 0)
    looked = jnp.zeros((8, pairs), F32)
    for q in range(n_dom):
        mine = wanted[q:q + 1]
        hit = (place[q:q + 1] == slot) & (mine > 0)
        lists = jnp.where(lane == q, jnp.sum(jnp.where(hit, leaf, 0), axis=1, keepdims=True), lists)
        rows = jnp.where(line == 0, place[q:q + 1], jnp.where(line == 1, mine.astype(F32), 0.0))
        here = as_bf16((iota((leaves, pairs), 0) == source_leaf) & (source_dom == q))
        looked += jnp.dot(rows.astype(BF16), here, preferred_element_type=F32)
    list_ref[...] = lists
    looked = looked.astype(I32)
    pairs_ref[0:1, :] = ids_ref[0:1, :]
    pairs_ref[1:2, :] = jnp.maximum((source_dom ^ me) - 1, 0) * SLOTS + looked[0:1]
    pairs_ref[2:3, :] = looked[1:2]
    pairs_ref[3:5, :] = local_ref[...]
    pairs_ref[5:6, :] = jnp.maximum((source_dom ^ me) - 1, 0) * leaves + source_leaf
    pairs_ref[6:8, :] = jnp.zeros((2, pairs), I32)


def start_copies(sems, *pairs):
    loads = [pltpu.make_async_copy(source, target, sems.at[n]) for n, (source, target) in enumerate(pairs)]
    for load in loads:
        load.start()
    return loads


def by_half(ref, b, half):
    rows = [jnp.broadcast_to(ref[pl.ds(b + at, 1), :], (8, LEAF)) for at in (0, half)]
    return jnp.where(iota((8, LEAF), 0) < 4, rows[0], rows[1])


def place_particles(n_sub, leaves, ordered, spans, leaf_idx, tiles, out_ref):
    off_ref, cnt_ref, start_ref = spans
    half = ordered.shape[0]
    lane = iota((8, LEAF), 1)

    def step(b, tails):
        block = ordered[b]
        new = []
        for e in range(n_sub):
            offset = by_half(off_ref.at[e], b, half)
            count = by_half(cnt_ref.at[e], b, half)
            first = by_half(start_ref.at[e], b, half)
            turned = (lane - offset) & (LEAF - 1)
            moved = lane_gather(block, (turned + first) & (LEAF - 1))
            low = offset & (LEAF - 1)
            taken = turned < count
            tail = jnp.where(taken & (lane >= low), moved, tails[e])
            tiles[leaf_idx[b, e], 0:4, :] = tail[0:4]
            tiles[leaf_idx[b + half, e], 4:8, :] = tail[4:8]
            fresh = jnp.where(taken & (lane < low), moved, 0.0)
            new.append(jnp.where(low + count >= LEAF, fresh, tail))
        return tuple(new)

    tails = lax.fori_loop(0, half, step, (jnp.zeros((8, LEAF), F32),) * n_sub, unroll=16)
    for e in range(n_sub):
        tiles[leaf_idx[half - 1, n_sub + e], 0:4, :] = tails[e][0:4]
        tiles[leaf_idx[2 * half - 1, n_sub + e], 4:8, :] = tails[e][4:8]
        for l in range(leaves):
            tile = tiles[e * (leaves + 1) + l]
            out_ref[e, 4 * l:4 * l + 4, :] = tile[0:4] + tile[4:8]


def regroup_kernel(
    n_sub, leaves, pos_hbm, mass_hbm, dest_hbm, near_ref, off_ref, cnt_ref, start_ref, inv_ref, leaf_vec,
    pos_ref, mass_ref, dest_ref, tiles, table, ordered, perm_ref, leaf_idx, sems
):
    blocks = dest_ref.shape[0]
    half = blocks // 2
    loads = start_copies(sems, (dest_hbm, dest_ref), (pos_hbm, pos_ref), (mass_hbm, mass_ref))
    tiles[...] = jnp.zeros_like(tiles)
    row = iota((LEAF, LEAF), 0)
    weights = jnp.concatenate([as_bf16(row <= iota((LEAF, LEAF), 1)), jnp.ones((LEAF, LEAF), BF16)], axis=1)
    earlier = as_bf16(iota((blocks, blocks), 1) < iota((blocks, blocks), 0))
    lane64 = iota((blocks, LEAF), 1)
    for load in loads:
        load.wait()
    dest = dest_ref[...]
    masks = [dest == e for e in range(n_sub)]
    ones_of = jnp.concatenate([as_bf16(m) for m in masks], axis=0)
    counts = jnp.dot(ones_of, weights, preferred_element_type=F32)
    start = jnp.zeros((blocks, LEAF), F32)
    place = jnp.zeros((blocks, LEAF), F32)
    leaf_of = jnp.zeros((blocks, LEAF), I32)
    for e in range(n_sub):
        inside = counts[e * blocks:(e + 1) * blocks, :LEAF]
        total = counts[e * blocks:(e + 1) * blocks, LEAF:]
        place = jnp.where(masks[e], inside - 1.0 + start, place)
        offset = jnp.dot(earlier, total.astype(BF16), preferred_element_type=F32).astype(I32)
        count = total.astype(I32)
        off_ref[e] = offset
        cnt_ref[e] = count
        start_ref[e] = start.astype(I32)
        base = e * (leaves + 1)
        leaf_of = jnp.where(lane64 == e, base + (offset >> 7), leaf_of)
        leaf_of = jnp.where(lane64 == n_sub + e, base + ((offset + count) >> 7), leaf_of)
        start = start + total
    leaf_vec[...] = leaf_of
    copy = pltpu.make_async_copy(leaf_vec, leaf_idx, sems.at[3])
    copy.start()
    perm_ref[...] = place.astype(I32)
    for b in range(blocks):
        at = b // half * 4
        table[b % half, at:at + 3, :] = pos_ref[:, b * LEAF:(b + 1) * LEAF]
        table[b % half, at + 3:at + 4, :] = mass_ref[b:b + 1, :]
    lane_rows = iota((16, LEAF), 1).astype(F32).astype(BF16)
    upper_half = iota((8, LEAF), 0) < 4

    def order(b, _):
        inverse = []
        for at in (b, b + half):
            onehot = as_bf16(row == perm_ref[pl.ds(at, 1), :])
            found = lax.dot_general(
                lane_rows, onehot, (((1,), (1,)), ((), ())), preferred_element_type=F32
            )[:8].astype(I32)
            inv_ref[pl.ds(at, 1), :] = found[:1]
            inverse.append(found)
        ordered[b] = lane_gather(table[b], jnp.where(upper_half, inverse[0], inverse[1]))
        return 0

    lax.fori_loop(0, half, order, 0, unroll=half)
    copy.wait()
    place_particles(n_sub, leaves, ordered, (off_ref, cnt_ref, start_ref), leaf_idx, tiles, near_ref)


def regroup(positions, masses, destinations, n_sub, leaves):
    count = positions.shape[1]
    blocks = count // LEAF
    spans = jax.ShapeDtypeStruct((n_sub, blocks, LEAF), I32)
    rows = jax.ShapeDtypeStruct((blocks, LEAF), I32)
    return pl.pallas_call(
        functools.partial(regroup_kernel, n_sub, leaves),
        out_shape=(jax.ShapeDtypeStruct((n_sub, leaves * 4, LEAF), F32), spans, spans, spans, rows, rows),
        in_specs=[hbm()] * 3,
        out_specs=(vmem(),) * 6,
        scratch_shapes=[
            pltpu.VMEM((3, count), F32),
            pltpu.VMEM((blocks, LEAF), F32),
            pltpu.VMEM((blocks, LEAF), I32),
            pltpu.VMEM((n_sub * (leaves + 1), 8, LEAF), F32),
            pltpu.VMEM((blocks // 2, 8, LEAF), F32),
            pltpu.VMEM((blocks // 2, 8, LEAF), F32),
            pltpu.VMEM((blocks, LEAF), I32),
            pltpu.SMEM((blocks, LEAF), I32),
            pltpu.SemaphoreType.DMA((4,)),
        ],
        compiler_params=params(),
        name="regroup",
    )(*in_hbm(positions, masses.reshape(blocks, LEAF), destinations.reshape(blocks, LEAF)))


def velocity_kernel(
    n_sub, n_dom, leaves, vel_hbm, reads_hbm, ids_hbm, local_hbm, off_ref, cnt_ref, start_ref, inv_ref, leaf_vec,
    far_ref, list_ref, pairs_ref, vel_ref, reads_ref, ids_ref, local_ref, tiles, table, ordered, leaf_idx, sems
):
    half = ordered.shape[0]
    loads = start_copies(
        sems, (vel_hbm, vel_ref), (leaf_vec, leaf_idx), (reads_hbm, reads_ref), (ids_hbm, ids_ref),
        (local_hbm, local_ref),
    )
    tiles[...] = jnp.zeros_like(tiles)
    table[...] = jnp.zeros_like(table)
    for load in loads:
        load.wait()
    plan_reads(n_dom, reads_ref, ids_ref, local_ref, list_ref, pairs_ref)
    for b in range(2 * half):
        at = b // half * 4
        table[b % half, at:at + 3, :] = vel_ref[:, b * LEAF:(b + 1) * LEAF]

    def order(b, _):
        ordered[b] = lane_gather(table[b], by_half(inv_ref, b, half))
        return 0

    lax.fori_loop(0, half, order, 0, unroll=8)
    place_particles(n_sub, leaves, ordered, (off_ref, cnt_ref, start_ref), leaf_idx, tiles, far_ref)


def regroup_velocities(velocities, reads, near_local, near_remote, tables, n_sub, leaves):
    count = velocities.shape[1]
    blocks = count // LEAF
    n_dom = reads.shape[0]
    return pl.pallas_call(
        functools.partial(velocity_kernel, n_sub, n_dom, leaves),
        out_shape=(
            jax.ShapeDtypeStruct((n_sub, leaves * 4, LEAF), F32),
            jax.ShapeDtypeStruct((SLOTS, LEAF), I32),
            jax.ShapeDtypeStruct((8, near_remote.shape[1]), I32),
        ),
        in_specs=[hbm()] * 4 + [vmem()] * 5,
        out_specs=(vmem(),) * 3,
        scratch_shapes=[
            pltpu.VMEM((3, count), F32),
            pltpu.VMEM(reads.shape, I32),
            pltpu.VMEM(near_remote.shape, I32),
            pltpu.VMEM(near_local.shape, I32),
            pltpu.VMEM((n_sub * (leaves + 1), 8, LEAF), F32),
            pltpu.VMEM((blocks // 2, 8, LEAF), F32),
            pltpu.VMEM((blocks // 2, 8, LEAF), F32),
            pltpu.SMEM((blocks, LEAF), I32),
            pltpu.SemaphoreType.DMA((5,)),
        ],
        compiler_params=params(),
        cost_estimate=pl.CostEstimate(flops=200 * n_sub * count, transcendentals=0, bytes_accessed=400 * count),
        name="regroup_velocities",
    )(*in_hbm(velocities, reads, near_remote, near_local), *tables)


UNROLL = 8


def spread_tiles(tile_of, count, wide_ref):
    group = iota((8, LEAF), 1) & ~15
    for k in range(16):
        for h in range(count):
            wide_ref[k, h] = lane_gather(tile_of(h), group + k)


def live_pairs(targets, sources, flags, target_mass, keys, source_mass, list_ref):
    pairs = targets.shape[1]
    spare = target_mass.shape[0]

    def filled(ids, mass):
        some = jnp.broadcast_to(mass[:, :1] > 0.0, (mass.shape[0], pairs))
        pick = as_bf16((iota((mass.shape[0], pairs), 0) == ids) & some)
        return jnp.dot(jnp.ones((8, mass.shape[0]), BF16), pick, preferred_element_type=F32)

    live = filled(targets, target_mass) * filled(keys, source_mass)
    if flags is not None:
        live = live * flags.astype(F32)
    row, col = iota((pairs, pairs), 0), iota((pairs, pairs), 1)
    place = jnp.dot(live.astype(BF16), as_bf16(row < col), preferred_element_type=F32).astype(I32)
    move = as_bf16((place[:1] == row) & (live[:1] > 0.0))
    line = iota((8, pairs), 0)
    rows = jnp.where(line == 0, targets.astype(F32), jnp.where(line == 1, sources.astype(F32), 1.0))
    moved = lax.dot_general(
        rows.astype(BF16), move, (((1,), (1,)), ((), ())), preferred_element_type=F32
    ).astype(I32)
    count = jnp.sum(live, axis=1, keepdims=True).astype(I32)
    moved = jnp.where((line == 0) & (moved[2:3] == 0), spare, moved)
    list_ref[...] = jnp.where(line == 2, count, moved)


def pair_loop(list_ref, here_ref, wide_ref, acc_ref):
    def pair(i):
        t = list_ref[0, i]
        s = list_ref[1, i]
        h, first = s >> 1, (s & 1) * 4
        here = [here_ref[t, c] for c in range(3)]
        sums = None
        for k in range(16):
            there = [jnp.broadcast_to(wide_ref[k, h, pl.ds(first + c, 1), :], (8, LEAF)) for c in range(4)]
            delta = [there[c] - here[c] for c in range(3)]
            dist = delta[0] * delta[0] + delta[1] * delta[1] + (delta[2] * delta[2] + softening)
            inv = lax.rsqrt(dist)
            weight = (there[3] * inv) * (inv * inv)
            terms = [weight * delta[c] for c in range(3)]
            sums = terms if sums is None else [sums[c] + terms[c] for c in range(3)]
            if k == 7:
                early, sums = sums, None
        for c in range(3):
            acc_ref[t, c] += sums[c] + early[c]

    def step(j, _):
        for u in range(UNROLL):
            pair(j * UNROLL + u)
        return 0

    lax.fori_loop(0, (list_ref[2, 0] + UNROLL - 1) // UNROLL, step, 0)


def local_kernel(ids_ref, src_ref, acc_ref, here_ref, wide_ref, list_vec, list_ref, sem):
    leaves = acc_ref.shape[0] - 1
    mass = src_ref[pl.ds(3, leaves, stride=4), :]
    live_pairs(ids_ref[3:4, :], ids_ref[4:5, :], None, mass, ids_ref[4:5, :], mass, list_vec)
    copy = pltpu.make_async_copy(list_vec, list_ref, sem)
    copy.start()
    spread_tiles(lambda h: src_ref[8 * h:8 * h + 8, :], leaves // 2, wide_ref)
    fold = iota((8, LEAF), 0) * 16 + (iota((8, LEAF), 1) & 15)
    for t in range(leaves):
        for c in range(3):
            line = src_ref[4 * t + c:4 * t + c + 1, :]
            here_ref[t, c] = lane_gather(jnp.broadcast_to(line, (8, LEAF)), fold)
    here_ref[leaves] = jnp.zeros((3, 8, LEAF), F32)
    acc_ref[...] = jnp.zeros_like(acc_ref)
    copy.wait()
    pair_loop(list_ref, here_ref, wide_ref, acc_ref)


def local_forces(ids, near):
    rows = near.shape[0]
    leaves = rows // 4
    pairs = ids.shape[1]
    assert pairs % UNROLL == 0
    work = pairs * LEAF * LEAF
    return pl.pallas_call(
        local_kernel,
        out_shape=(
            jax.ShapeDtypeStruct((leaves + 1, 4, 8, LEAF), F32),
            jax.ShapeDtypeStruct((leaves + 1, 3, 8, LEAF), F32),
        ),
        in_specs=[vmem(), vmem()],
        out_specs=(vmem(), vmem()),
        scratch_shapes=[
            pltpu.VMEM((16, rows // 8, 8, LEAF), F32),
            pltpu.VMEM((8, pairs), I32),
            pltpu.SMEM((8, pairs), I32),
            pltpu.SemaphoreType.DMA,
        ],
        compiler_params=params(),
        cost_estimate=pl.CostEstimate(flops=18 * work, transcendentals=work, bytes_accessed=8 * rows * LEAF),
        name="local_forces",
    )(ids, near)


def three_parts(x):
    high = x.astype(BF16)
    rest = x - high.astype(F32)
    middle = rest.astype(BF16)
    return [high, middle, (rest - middle.astype(F32)).astype(BF16)]


def unpack_sums(acc_refs, leaves):
    source, target = iota((LEAF, LEAF), 0), iota((LEAF, LEAF), 1)
    parts, picks = [], []
    for s in range(8):
        lines = [ref.reshape((leaves + 1) * 32, LEAF)[pl.ds(s, leaves * 4, stride=8), :] for ref in acc_refs]
        pick = as_bf16(((source & 15) == (target & 15)) & ((target >> 4) == s))
        parts += three_parts(sum(lines[1:], lines[0]))
        picks += [pick] * 3
    return jnp.dot(
        jnp.concatenate(parts, axis=1), jnp.concatenate(picks, axis=0), preferred_element_type=F32
    )


def remote_kernel(n_dom, leaf_list, pairs_ref, tgt_ref, vel_ref, local_ref, here_ref, *rest):
    src_refs = rest[:n_dom - 1]
    (accel_ref, kicked_ref, leaf_ref, chosen_ref, wide_ref, acc_ref, list_vec, list_ref,
     sems) = rest[n_dom - 1:]
    me = lax.axis_index("dom")
    load = pltpu.make_async_copy(leaf_list, leaf_ref, sems.at[0])
    load.start()
    leaves = acc_ref.shape[0] - 1
    acc_ref[...] = jnp.zeros_like(acc_ref)
    slots = (n_dom - 1) * SLOTS
    live_pairs(
        pairs_ref[0:1, :], pairs_ref[1:2, :], pairs_ref[2:3, :], tgt_ref[pl.ds(3, leaves, stride=4), :],
        pairs_ref[5:6, :], jnp.concatenate([ref[:, 3, :] for ref in src_refs], axis=0), list_vec,
    )
    copy = pltpu.make_async_copy(list_vec, list_ref, sems.at[1])
    copy.start()
    load.wait()
    for k in range(1, n_dom):
        for j in range(SLOTS):
            at = 4 * ((k - 1) * SLOTS + j)
            chosen_ref[at:at + 4, :] = src_refs[k - 1][leaf_ref[j, me ^ k]]
    spread_tiles(lambda h: chosen_ref[8 * h:8 * h + 8, :], slots // 2, wide_ref)
    copy.wait()
    pair_loop(list_ref, here_ref, wide_ref, acc_ref)
    total = gravity * unpack_sums([local_ref, acc_ref], leaves)
    first = iota((8, LEAF), 0) < 4
    per = vel_ref.shape[1]
    for h in range(leaves // 2):
        rows = slice(8 * h, 8 * h + 8)
        mass = [jnp.broadcast_to(tgt_ref[8 * h + r:8 * h + r + 1, :], (8, LEAF)) for r in (3, 7)]
        accel = jnp.where(jnp.where(first, mass[0], mass[1]) > 0.0, total[rows], 0.0)
        kicked = jnp.concatenate(
            [vel_ref[r // per, r % per:r % per + 4, :] for r in (8 * h, 8 * h + 4)], axis=0
        ) + kick_time * accel
        for u in range(2):
            lanes = slice((2 * h + u) * LEAF, (2 * h + u + 1) * LEAF)
            accel_ref[:, lanes] = accel[4 * u:4 * u + 3]
            kicked_ref[:, lanes] = kicked[4 * u:4 * u + 3]


def remote_forces(lists, pairs, near, vel, local, here, arrived):
    n_dom = len(arrived) + 1
    rows = near.shape[0]
    leaves = rows // 4
    slots = (n_dom - 1) * SLOTS
    work = pairs.shape[1] * LEAF * LEAF
    assert pairs.shape[1] % UNROLL == 0
    out = jax.ShapeDtypeStruct((3, leaves * LEAF), F32)
    return pl.pallas_call(
        functools.partial(remote_kernel, n_dom),
        out_shape=(out, out),
        in_specs=[vmem()] * (5 + n_dom),
        out_specs=(vmem(), vmem()),
        scratch_shapes=[
            pltpu.SMEM(lists.shape, I32),
            pltpu.VMEM((slots * 4, LEAF), F32),
            pltpu.VMEM((16, slots // 2, 8, LEAF), F32),
            pltpu.VMEM((leaves + 1, 4, 8, LEAF), F32),
            pltpu.VMEM(pairs.shape, I32),
            pltpu.SMEM(pairs.shape, I32),
            pltpu.SemaphoreType.DMA((2,)),
        ],
        compiler_params=params(),
        cost_estimate=pl.CostEstimate(flops=18 * work, transcendentals=work, bytes_accessed=24 * rows * LEAF),
        name="remote_forces",
    )(lists, pairs, near, vel, local, here, *arrived)


def on_device(positions, masses, velocities, destinations, readers, near_local, near_remote):
    n_sub = lax.axis_size("sub")
    n_dom = lax.axis_size("dom")
    count = positions.shape[1]
    capacity = 5 * count // (4 * n_sub)
    leaves = capacity // LEAF
    reads = readers.reshape(n_dom, n_dom, readers.shape[3])
    near, *tables = regroup(positions, masses, destinations, n_sub, leaves)
    near = lax.all_to_all(near, "sub", split_axis=0, concat_axis=0, tiled=True)
    far, lists, pairs = regroup_velocities(velocities, reads, near_local, near_remote, tables, n_sub, leaves)
    near, far, lists, pairs = lax.optimization_barrier((near, far, lists, pairs))
    whole = near.reshape(n_sub * leaves, 4, LEAF)
    arrived = [lax.ppermute(whole, "dom", [(i, i ^ k) for i in range(n_dom)]) for k in range(1, n_dom)]
    far = lax.all_to_all(far, "sub", split_axis=0, concat_axis=0, tiled=True)
    near = near.reshape(n_sub * leaves * 4, LEAF)
    local, here = local_forces(pairs, near)
    return remote_forces(lists, pairs, near, far, local, here, arrived)


def solution(mesh):
    in_specs = (
        P(None, ("dom", "sub")),
        P(("dom", "sub")),
        P(None, ("dom", "sub")),
        P(("dom", "sub"), None),
        P(None, None, "sub", None),
        P(None, ("dom", "sub")),
        P(None, ("dom", "sub")),
    )
    out_specs = (P(None, ("dom", "sub")), P(None, ("dom", "sub")))
    return jax.shard_map(
        on_device, mesh=mesh, in_specs=in_specs, out_specs=out_specs, check_vma=False
    )
```

```python
import functools

import jax
import jax.numpy as jnp
from jax import lax
from jax.experimental import pallas as pl
from jax.experimental.pallas import tpu as pltpu
from jax.sharding import PartitionSpec as P

SLOTS = 32
LEAF = 128

softening = 0.01
gravity = 4.0
kick_time = 0.5

VMEM_LIMIT = 48 << 20
F32 = jnp.float32
I32 = jnp.int32
BF16 = jnp.bfloat16


def vmem():
    return pl.BlockSpec(memory_space=pltpu.VMEM)


def smem():
    return pl.BlockSpec(memory_space=pltpu.SMEM)


def hbm():
    return pl.BlockSpec(memory_space=pltpu.HBM)


def in_hbm(*arrays):
    return [pltpu.with_memory_space_constraint(x, pltpu.MemorySpace.HBM) for x in arrays]


def params():
    return pltpu.CompilerParams(vmem_limit_bytes=VMEM_LIMIT)


def lane_gather(tile, index):
    return jnp.take_along_axis(tile, index, axis=1, mode="promise_in_bounds")


def iota(shape, dim):
    return lax.broadcasted_iota(I32, shape, dim)


def as_bf16(condition):
    return jnp.where(condition, 1.0, 0.0).astype(BF16)


def plan_reads(n_dom, reads_ref, ids_ref, local_ref, list_ref, pairs_ref):
    me = lax.axis_index("dom")
    leaves = reads_ref.shape[2]
    pairs = ids_ref.shape[1]
    lower = as_bf16(iota((leaves, leaves), 0) < iota((leaves, leaves), 1))
    wanted = reads_ref[me]
    flags = wanted.astype(F32).astype(BF16)
    place = jnp.minimum(jnp.dot(flags, lower, preferred_element_type=F32), SLOTS - 1.0)
    slot = iota((SLOTS, leaves), 0).astype(F32)
    leaf = iota((SLOTS, leaves), 1)
    lane = iota((SLOTS, LEAF), 1)
    lists = jnp.zeros((SLOTS, LEAF), I32)
    source_dom, source_leaf = ids_ref[1:2, :], ids_ref[2:3, :]
    line = iota((8, leaves), 0)
    looked = jnp.zeros((8, pairs), F32)
    for q in range(n_dom):
        mine = wanted[q:q + 1]
        hit = (place[q:q + 1] == slot) & (mine > 0)
        lists = jnp.where(lane == q, jnp.sum(jnp.where(hit, leaf, 0), axis=1, keepdims=True), lists)
        rows = jnp.where(line == 0, place[q:q + 1], jnp.where(line == 1, mine.astype(F32), 0.0))
        here = as_bf16((iota((leaves, pairs), 0) == source_leaf) & (source_dom == q))
        looked += jnp.dot(rows.astype(BF16), here, preferred_element_type=F32)
    list_ref[...] = lists
    looked = looked.astype(I32)
    pairs_ref[0:1, :] = ids_ref[0:1, :]
    pairs_ref[1:2, :] = jnp.maximum((source_dom ^ me) - 1, 0) * SLOTS + looked[0:1]
    pairs_ref[2:3, :] = looked[1:2]
    pairs_ref[3:5, :] = local_ref[...]
    pairs_ref[5:6, :] = jnp.maximum((source_dom ^ me) - 1, 0) * leaves + source_leaf
    pairs_ref[6:8, :] = jnp.zeros((2, pairs), I32)


def start_copies(sems, *pairs):
    loads = [pltpu.make_async_copy(source, target, sems.at[n]) for n, (source, target) in enumerate(pairs)]
    for load in loads:
        load.start()
    return loads


def by_half(ref, b, half):
    rows = [jnp.broadcast_to(ref[pl.ds(b + at, 1), :], (8, LEAF)) for at in (0, half)]
    return jnp.where(iota((8, LEAF), 0) < 4, rows[0], rows[1])


def place_particles(n_sub, leaves, ordered, spans, leaf_idx, tiles, out_ref):
    off_ref, cnt_ref, start_ref = spans
    half = ordered.shape[0]
    lane = iota((8, LEAF), 1)

    def step(b, tails):
        block = ordered[b]
        new = []
        for e in range(n_sub):
            offset = by_half(off_ref.at[e], b, half)
            count = by_half(cnt_ref.at[e], b, half)
            first = by_half(start_ref.at[e], b, half)
            turned = (lane - offset) & (LEAF - 1)
            moved = lane_gather(block, (turned + first) & (LEAF - 1))
            low = offset & (LEAF - 1)
            taken = turned < count
            tail = jnp.where(taken & (lane >= low), moved, tails[e])
            tiles[leaf_idx[b, e], 0:4, :] = tail[0:4]
            tiles[leaf_idx[b + half, e], 4:8, :] = tail[4:8]
            fresh = jnp.where(taken & (lane < low), moved, 0.0)
            new.append(jnp.where(low + count >= LEAF, fresh, tail))
        return tuple(new)

    tails = lax.fori_loop(0, half, step, (jnp.zeros((8, LEAF), F32),) * n_sub, unroll=half)
    for e in range(n_sub):
        tiles[leaf_idx[half - 1, n_sub + e], 0:4, :] = tails[e][0:4]
        tiles[leaf_idx[2 * half - 1, n_sub + e], 4:8, :] = tails[e][4:8]
        for l in range(leaves):
            tile = tiles[e * (leaves + 1) + l]
            out_ref[e, 4 * l:4 * l + 4, :] = tile[0:4] + tile[4:8]


def regroup_kernel(
    n_sub, leaves, pos_hbm, mass_hbm, dest_hbm, near_ref, off_ref, cnt_ref, start_ref, inv_ref, leaf_vec,
    pos_ref, mass_ref, dest_ref, tiles, table, ordered, perm_ref, leaf_idx, sems
):
    blocks = dest_ref.shape[0]
    half = blocks // 2
    loads = start_copies(sems, (dest_hbm, dest_ref), (pos_hbm, pos_ref), (mass_hbm, mass_ref))
    tiles[...] = jnp.zeros_like(tiles)
    row = iota((LEAF, LEAF), 0)
    weights = jnp.concatenate([as_bf16(row <= iota((LEAF, LEAF), 1)), jnp.ones((LEAF, LEAF), BF16)], axis=1)
    earlier = as_bf16(iota((blocks, blocks), 1) < iota((blocks, blocks), 0))
    lane64 = iota((blocks, LEAF), 1)
    for load in loads:
        load.wait()
    dest = dest_ref[...]
    masks = [dest == e for e in range(n_sub)]
    ones_of = jnp.concatenate([as_bf16(m) for m in masks], axis=0)
    counts = jnp.dot(ones_of, weights, preferred_element_type=F32)
    start = jnp.zeros((blocks, LEAF), F32)
    place = jnp.zeros((blocks, LEAF), F32)
    leaf_of = jnp.zeros((blocks, LEAF), I32)
    for e in range(n_sub):
        inside = counts[e * blocks:(e + 1) * blocks, :LEAF]
        total = counts[e * blocks:(e + 1) * blocks, LEAF:]
        place = jnp.where(masks[e], inside - 1.0 + start, place)
        offset = jnp.dot(earlier, total.astype(BF16), preferred_element_type=F32).astype(I32)
        count = total.astype(I32)
        off_ref[e] = offset
        cnt_ref[e] = count
        start_ref[e] = start.astype(I32)
        base = e * (leaves + 1)
        leaf_of = jnp.where(lane64 == e, base + (offset >> 7), leaf_of)
        leaf_of = jnp.where(lane64 == n_sub + e, base + ((offset + count) >> 7), leaf_of)
        start = start + total
    leaf_vec[...] = leaf_of
    copy = pltpu.make_async_copy(leaf_vec, leaf_idx, sems.at[3])
    copy.start()
    perm_ref[...] = place.astype(I32)
    for b in range(blocks):
        at = b // half * 4
        table[b % half, at:at + 3, :] = pos_ref[:, b * LEAF:(b + 1) * LEAF]
        table[b % half, at + 3:at + 4, :] = mass_ref[b:b + 1, :]
    lane_rows = iota((16, LEAF), 1).astype(F32).astype(BF16)
    upper_half = iota((8, LEAF), 0) < 4

    def order(b, _):
        inverse = []
        for at in (b, b + half):
            onehot = as_bf16(row == perm_ref[pl.ds(at, 1), :])
            found = lax.dot_general(
                lane_rows, onehot, (((1,), (1,)), ((), ())), preferred_element_type=F32
            )[:8].astype(I32)
            inv_ref[pl.ds(at, 1), :] = found[:1]
            inverse.append(found)
        ordered[b] = lane_gather(table[b], jnp.where(upper_half, inverse[0], inverse[1]))
        return 0

    lax.fori_loop(0, half, order, 0, unroll=half)
    copy.wait()
    place_particles(n_sub, leaves, ordered, (off_ref, cnt_ref, start_ref), leaf_idx, tiles, near_ref)


def regroup(positions, masses, destinations, n_sub, leaves):
    count = positions.shape[1]
    blocks = count // LEAF
    spans = jax.ShapeDtypeStruct((n_sub, blocks, LEAF), I32)
    rows = jax.ShapeDtypeStruct((blocks, LEAF), I32)
    return pl.pallas_call(
        functools.partial(regroup_kernel, n_sub, leaves),
        out_shape=(jax.ShapeDtypeStruct((n_sub, leaves * 4, LEAF), F32), spans, spans, spans, rows, rows),
        in_specs=[hbm()] * 3,
        out_specs=(vmem(),) * 6,
        scratch_shapes=[
            pltpu.VMEM((3, count), F32),
            pltpu.VMEM((blocks, LEAF), F32),
            pltpu.VMEM((blocks, LEAF), I32),
            pltpu.VMEM((n_sub * (leaves + 1), 8, LEAF), F32),
            pltpu.VMEM((blocks // 2, 8, LEAF), F32),
            pltpu.VMEM((blocks // 2, 8, LEAF), F32),
            pltpu.VMEM((blocks, LEAF), I32),
            pltpu.SMEM((blocks, LEAF), I32),
            pltpu.SemaphoreType.DMA((4,)),
        ],
        compiler_params=params(),
        name="regroup",
    )(*in_hbm(positions, masses.reshape(blocks, LEAF), destinations.reshape(blocks, LEAF)))


def velocity_kernel(
    n_sub, n_dom, leaves, vel_hbm, reads_hbm, ids_hbm, local_hbm, off_ref, cnt_ref, start_ref, inv_ref, leaf_vec,
    far_ref, list_ref, pairs_ref, vel_ref, reads_ref, ids_ref, local_ref, tiles, table, ordered, leaf_idx, sems
):
    half = ordered.shape[0]
    loads = start_copies(
        sems, (vel_hbm, vel_ref), (leaf_vec, leaf_idx), (reads_hbm, reads_ref), (ids_hbm, ids_ref),
        (local_hbm, local_ref),
    )
    tiles[...] = jnp.zeros_like(tiles)
    table[...] = jnp.zeros_like(table)
    for load in loads:
        load.wait()
    plan_reads(n_dom, reads_ref, ids_ref, local_ref, list_ref, pairs_ref)
    for b in range(2 * half):
        at = b // half * 4
        table[b % half, at:at + 3, :] = vel_ref[:, b * LEAF:(b + 1) * LEAF]

    def order(b, _):
        ordered[b] = lane_gather(table[b], by_half(inv_ref, b, half))
        return 0

    lax.fori_loop(0, half, order, 0, unroll=8)
    place_particles(n_sub, leaves, ordered, (off_ref, cnt_ref, start_ref), leaf_idx, tiles, far_ref)


def regroup_velocities(velocities, reads, near_local, near_remote, tables, n_sub, leaves):
    count = velocities.shape[1]
    blocks = count // LEAF
    n_dom = reads.shape[0]
    return pl.pallas_call(
        functools.partial(velocity_kernel, n_sub, n_dom, leaves),
        out_shape=(
            jax.ShapeDtypeStruct((n_sub, leaves * 4, LEAF), F32),
            jax.ShapeDtypeStruct((SLOTS, LEAF), I32),
            jax.ShapeDtypeStruct((8, near_remote.shape[1]), I32),
        ),
        in_specs=[hbm()] * 4 + [vmem()] * 5,
        out_specs=(vmem(),) * 3,
        scratch_shapes=[
            pltpu.VMEM((3, count), F32),
            pltpu.VMEM(reads.shape, I32),
            pltpu.VMEM(near_remote.shape, I32),
            pltpu.VMEM(near_local.shape, I32),
            pltpu.VMEM((n_sub * (leaves + 1), 8, LEAF), F32),
            pltpu.VMEM((blocks // 2, 8, LEAF), F32),
            pltpu.VMEM((blocks // 2, 8, LEAF), F32),
            pltpu.SMEM((blocks, LEAF), I32),
            pltpu.SemaphoreType.DMA((5,)),
        ],
        compiler_params=params(),
        cost_estimate=pl.CostEstimate(flops=200 * n_sub * count, transcendentals=0, bytes_accessed=400 * count),
        name="regroup_velocities",
    )(*in_hbm(velocities, reads, near_remote, near_local), *tables)


UNROLL = 8
HEAD = 8


def spread_tiles(tile_of, count, wide_ref):
    group = iota((8, LEAF), 1) & ~15
    for k in range(16):
        for h in range(count):
            wide_ref[k, h] = lane_gather(tile_of(h), group + k)


def live_pairs(targets, sources, flags, target_mass, keys, source_mass, list_ref):
    pairs = targets.shape[1]
    spare = target_mass.shape[0]

    def filled(ids, mass):
        some = jnp.broadcast_to(mass[:, :1] > 0.0, (mass.shape[0], pairs))
        pick = as_bf16((iota((mass.shape[0], pairs), 0) == ids) & some)
        return jnp.dot(jnp.ones((8, mass.shape[0]), BF16), pick, preferred_element_type=F32)

    live = filled(targets, target_mass) * filled(keys, source_mass)
    if flags is not None:
        live = live * flags.astype(F32)
    live = jnp.where(iota((8, pairs), 1) < HEAD, 0.0, live)
    row, col = iota((pairs, pairs), 0), iota((pairs, pairs), 1)
    place = jnp.dot(live.astype(BF16), as_bf16(row < col), preferred_element_type=F32).astype(I32)
    move = as_bf16((place[:1] == row) & (live[:1] > 0.0))
    line = iota((8, pairs), 0)
    rows = jnp.where(line == 0, targets.astype(F32), jnp.where(line == 1, sources.astype(F32), 1.0))
    moved = lax.dot_general(
        rows.astype(BF16), move, (((1,), (1,)), ((), ())), preferred_element_type=F32
    ).astype(I32)
    count = jnp.sum(live, axis=1, keepdims=True).astype(I32)
    moved = jnp.where((line == 0) & (moved[2:3] == 0), spare, moved)
    list_ref[...] = jnp.where(line == 2, count, moved)


def pair_loop(head_of, copy, list_ref, here_ref, wide_ref, acc_ref):
    def pair(t, s):
        h, first = s >> 1, (s & 1) * 4
        here = [here_ref[t, c] for c in range(3)]
        sums = None
        for k in range(16):
            there = [jnp.broadcast_to(wide_ref[k, h, pl.ds(first + c, 1), :], (8, LEAF)) for c in range(4)]
            delta = [there[c] - here[c] for c in range(3)]
            dist = delta[0] * delta[0] + delta[1] * delta[1] + (delta[2] * delta[2] + softening)
            inv = lax.rsqrt(dist)
            weight = (there[3] * inv) * (inv * inv)
            terms = [weight * delta[c] for c in range(3)]
            sums = terms if sums is None else [sums[c] + terms[c] for c in range(3)]
            if k == 7:
                early, sums = sums, None
        for c in range(3):
            acc_ref[t, c] += sums[c] + early[c]

    def step(j, _):
        for u in range(UNROLL):
            pair(list_ref[0, j * UNROLL + u], list_ref[1, j * UNROLL + u])
        return 0

    for i in range(HEAD):
        pair(*head_of(i))
    copy.wait()
    lax.fori_loop(0, (list_ref[2, 0] + UNROLL - 1) // UNROLL, step, 0)


def local_kernel(ids_ref, src_ref, acc_ref, here_ref, wide_ref, list_vec, list_ref, raw_ref, sems):
    raw = pltpu.make_async_copy(ids_ref, raw_ref, sems.at[1])
    raw.start()
    leaves = acc_ref.shape[0] - 1
    mass = src_ref[pl.ds(3, leaves, stride=4), :]
    live_pairs(ids_ref[3:4, :], ids_ref[4:5, :], None, mass, ids_ref[4:5, :], mass, list_vec)
    copy = pltpu.make_async_copy(list_vec, list_ref, sems.at[0])
    copy.start()
    spread_tiles(lambda h: src_ref[8 * h:8 * h + 8, :], leaves // 2, wide_ref)
    fold = iota((8, LEAF), 0) * 16 + (iota((8, LEAF), 1) & 15)
    for t in range(leaves):
        for c in range(3):
            line = src_ref[4 * t + c:4 * t + c + 1, :]
            here_ref[t, c] = lane_gather(jnp.broadcast_to(line, (8, LEAF)), fold)
    here_ref[leaves] = jnp.zeros((3, 8, LEAF), F32)
    acc_ref[...] = jnp.zeros_like(acc_ref)
    raw.wait()
    pair_loop(lambda i: (raw_ref[3, i], raw_ref[4, i]), copy, list_ref, here_ref, wide_ref, acc_ref)


def local_forces(ids, near):
    rows = near.shape[0]
    leaves = rows // 4
    pairs = ids.shape[1]
    assert pairs % UNROLL == 0
    work = pairs * LEAF * LEAF
    return pl.pallas_call(
        local_kernel,
        out_shape=(
            jax.ShapeDtypeStruct((leaves + 1, 4, 8, LEAF), F32),
            jax.ShapeDtypeStruct((leaves + 1, 3, 8, LEAF), F32),
        ),
        in_specs=[vmem(), vmem()],
        out_specs=(vmem(), vmem()),
        scratch_shapes=[
            pltpu.VMEM((16, rows // 8, 8, LEAF), F32),
            pltpu.VMEM((8, pairs), I32),
            pltpu.SMEM((8, pairs), I32),
            pltpu.SMEM((8, pairs), I32),
            pltpu.SemaphoreType.DMA((2,)),
        ],
        compiler_params=params(),
        cost_estimate=pl.CostEstimate(flops=18 * work, transcendentals=work, bytes_accessed=8 * rows * LEAF),
        name="local_forces",
    )(ids, near)


def three_parts(x):
    high = x.astype(BF16)
    rest = x - high.astype(F32)
    middle = rest.astype(BF16)
    return [high, middle, (rest - middle.astype(F32)).astype(BF16)]


def unpack_sums(acc_refs, leaves):
    source, target = iota((LEAF, LEAF), 0), iota((LEAF, LEAF), 1)
    parts, picks = [], []
    for s in range(8):
        lines = [ref.reshape((leaves + 1) * 32, LEAF)[pl.ds(s, leaves * 4, stride=8), :] for ref in acc_refs]
        pick = as_bf16(((source & 15) == (target & 15)) & ((target >> 4) == s))
        parts += three_parts(sum(lines[1:], lines[0]))
        picks += [pick] * 3
    return jnp.dot(
        jnp.concatenate(parts, axis=1), jnp.concatenate(picks, axis=0), preferred_element_type=F32
    )


def remote_kernel(n_dom, leaf_list, pairs_ref, tgt_ref, vel_ref, local_ref, here_ref, *rest):
    src_refs = rest[:n_dom - 1]
    (accel_ref, kicked_ref, leaf_ref, chosen_ref, wide_ref, acc_ref, list_vec, list_ref,
     raw_ref, sems) = rest[n_dom - 1:]
    me = lax.axis_index("dom")
    load = pltpu.make_async_copy(leaf_list, leaf_ref, sems.at[0])
    load.start()
    raw = pltpu.make_async_copy(pairs_ref, raw_ref, sems.at[2])
    raw.start()
    leaves = acc_ref.shape[0] - 1
    acc_ref[...] = local_ref[...]
    slots = (n_dom - 1) * SLOTS
    live_pairs(
        pairs_ref[0:1, :], pairs_ref[1:2, :], pairs_ref[2:3, :], tgt_ref[pl.ds(3, leaves, stride=4), :],
        pairs_ref[5:6, :], jnp.concatenate([ref[:, 3, :] for ref in src_refs], axis=0), list_vec,
    )
    copy = pltpu.make_async_copy(list_vec, list_ref, sems.at[1])
    copy.start()
    load.wait()
    for k in range(1, n_dom):
        for j in range(SLOTS):
            at = 4 * ((k - 1) * SLOTS + j)
            chosen_ref[at:at + 4, :] = src_refs[k - 1][leaf_ref[j, me ^ k]]
    spread_tiles(lambda h: chosen_ref[8 * h:8 * h + 8, :], slots // 2, wide_ref)
    raw.wait()
    pair_loop(
        lambda i: (jnp.where(raw_ref[2, i] > 0, raw_ref[0, i], leaves), raw_ref[1, i]),
        copy, list_ref, here_ref, wide_ref, acc_ref,
    )
    total = gravity * unpack_sums([acc_ref], leaves)
    first = iota((8, LEAF), 0) < 4
    per = vel_ref.shape[1]
    for h in range(leaves // 2):
        rows = slice(8 * h, 8 * h + 8)
        mass = [jnp.broadcast_to(tgt_ref[8 * h + r:8 * h + r + 1, :], (8, LEAF)) for r in (3, 7)]
        accel = jnp.where(jnp.where(first, mass[0], mass[1]) > 0.0, total[rows], 0.0)
        kicked = jnp.concatenate(
            [vel_ref[r // per, r % per:r % per + 4, :] for r in (8 * h, 8 * h + 4)], axis=0
        ) + kick_time * accel
        for u in range(2):
            lanes = slice((2 * h + u) * LEAF, (2 * h + u + 1) * LEAF)
            accel_ref[:, lanes] = accel[4 * u:4 * u + 3]
            kicked_ref[:, lanes] = kicked[4 * u:4 * u + 3]


def remote_forces(lists, pairs, near, vel, local, here, arrived):
    n_dom = len(arrived) + 1
    rows = near.shape[0]
    leaves = rows // 4
    slots = (n_dom - 1) * SLOTS
    work = pairs.shape[1] * LEAF * LEAF
    assert pairs.shape[1] % UNROLL == 0
    out = jax.ShapeDtypeStruct((3, leaves * LEAF), F32)
    return pl.pallas_call(
        functools.partial(remote_kernel, n_dom),
        out_shape=(out, out),
        in_specs=[vmem()] * (5 + n_dom),
        out_specs=(vmem(), vmem()),
        scratch_shapes=[
            pltpu.SMEM(lists.shape, I32),
            pltpu.VMEM((slots * 4, LEAF), F32),
            pltpu.VMEM((16, slots // 2, 8, LEAF), F32),
            pltpu.VMEM((leaves + 1, 4, 8, LEAF), F32),
            pltpu.VMEM(pairs.shape, I32),
            pltpu.SMEM(pairs.shape, I32),
            pltpu.SMEM(pairs.shape, I32),
            pltpu.SemaphoreType.DMA((3,)),
        ],
        compiler_params=params(),
        cost_estimate=pl.CostEstimate(flops=18 * work, transcendentals=work, bytes_accessed=24 * rows * LEAF),
        name="remote_forces",
    )(lists, pairs, near, vel, local, here, *arrived)


def on_device(positions, masses, velocities, destinations, readers, near_local, near_remote):
    n_sub = lax.axis_size("sub")
    n_dom = lax.axis_size("dom")
    count = positions.shape[1]
    capacity = 5 * count // (4 * n_sub)
    leaves = capacity // LEAF
    reads = readers.reshape(n_dom, n_dom, readers.shape[3])
    near, *tables = regroup(positions, masses, destinations, n_sub, leaves)
    near = lax.all_to_all(near, "sub", split_axis=0, concat_axis=0, tiled=True)
    far, lists, pairs = regroup_velocities(velocities, reads, near_local, near_remote, tables, n_sub, leaves)
    near, far, lists, pairs = lax.optimization_barrier((near, far, lists, pairs))
    whole = near.reshape(n_sub * leaves, 4, LEAF)
    arrived = [lax.ppermute(whole, "dom", [(i, i ^ k) for i in range(n_dom)]) for k in range(1, n_dom)]
    far = lax.all_to_all(far, "sub", split_axis=0, concat_axis=0, tiled=True)
    near = near.reshape(n_sub * leaves * 4, LEAF)
    local, here = local_forces(pairs, near)
    return remote_forces(lists, pairs, near, far, local, here, arrived)


def solution(mesh):
    in_specs = (
        P(None, ("dom", "sub")),
        P(("dom", "sub")),
        P(None, ("dom", "sub")),
        P(("dom", "sub"), None),
        P(None, None, "sub", None),
        P(None, ("dom", "sub")),
        P(None, ("dom", "sub")),
    )
    out_specs = (P(None, ("dom", "sub")), P(None, ("dom", "sub")))
    return jax.shard_map(
        on_device, mesh=mesh, in_specs=in_specs, out_specs=out_specs, check_vma=False
    )
```
